768 devices in a mesh: mem: 32 (over y, x_hi, core), tile: 24 (over z, x_lo).
Axes of the slice: x: 4 (x_hi: 2, x_lo: 2; x = x_hi * 2 + x_lo), y: 8, z: 12, core: 2. Of those that a mesh axis runs over, the one named last changes fastest.
Arguments:
- alpha_fields: float32 [96, 768, 768], P('mem', 'tile'), may hold values from -6 to 6
- static_control: float32 [4, 768, 768], P(None, 'tile'), as said below
- perturbations: bfloat16 [96, 4, 768, 768], P('mem', None, 'tile'), may hold values from -6 to 6
- coef_table: float32 [8], replicated, may hold values from 0.12 to 0.25
- coef_class: int32 [768, 768], P('tile'), may hold values from 0 to 7
- obs_cells: int32 [24, 4096], P('tile'), may hold values from 0 to 98303
- obs_counts: int32 [24], P('tile'), may hold values from 2048 to 4096, as said below
- innovations: float32 [24, 4096], P('tile'), as said below
- obs_weights: float32 [24, 4096], P('tile'), may hold values from 10 to 100
Outputs:
- grad_alpha: float32 [96, 768, 768], P('mem', 'tile')
- grad_static: float32 [4, 768, 768], P(None, 'tile')
The draws below stay inside these ranges and needn't reach their ends.
Inputs may be any that keep to these rules, and one draw needn't show every extreme that they name: `obs_counts`: at most 4096, and some strip uses all 4096 slots in every draw. `static_control`: real values. `innovations`: real values.
All inputs are finite; a program needn't handle non-finite values.
Results may differ from the reference program's by a relative error of at most 0.0004.
Values sent between devices are 32-bit elements; how exact they have to be, the bound alone decides.
A program may use at most 32 MiB of HBM per device.

```python
import math
import jax
import jax.numpy as jnp
from jax import lax

CX = 32
NY = 768
NVAR = 4
STEPS = 4
CLASSES = 8
OBS_TILE = 4096
MEMBERS = 96
TILES = 24
NX = 768


def draw_obs_counts(key, part):
    first_key, second_key = jax.random.split(jax.random.fold_in(key, 17))
    counts = jax.random.randint(first_key, (TILES,), OBS_TILE // 2, OBS_TILE + 1)
    chosen = jax.random.randint(second_key, (), 0, TILES)
    return jnp.where(jnp.arange(TILES) == chosen, OBS_TILE, counts).astype(jnp.int32)


def draw_static_control(key, part):
    rough = jax.random.truncated_normal(jax.random.fold_in(key, 23), -6.0, 6.0, (NVAR, NX, NY), jnp.float32)
    return rough.astype(jnp.float32)


def draw_innovations(key, part):
    rough = jax.random.truncated_normal(jax.random.fold_in(key, 29), -6.0, 6.0, (TILES, OBS_TILE), jnp.float32)
    return rough.astype(jnp.float32)


def with_ends(result, stream_key, least, largest):
    place = [jax.random.randint(jax.random.fold_in(stream_key, axis), (), 0, length) for axis, length in enumerate(result.shape)]
    main_axis = result.shape.index(max(result.shape))
    beside = place[:main_axis] + [(place[main_axis] + 1) % result.shape[main_axis]] + place[main_axis + 1:]
    return result.at[tuple(place)].set(least).at[tuple(beside)].set(largest)


def steps_of(stream_key, dims, shards, low, largest):
    gain = 1.0
    for axis_at, parts in shards:
        draws = jax.random.uniform(jax.random.fold_in(jax.random.fold_in(stream_key, 6), axis_at), (parts,), jnp.float32, low / len(shards), largest / len(shards))
        gain = gain * jnp.repeat(jnp.exp(draws), dims[axis_at] // parts).reshape((-1,) + (1,) * (len(dims) - 1 - axis_at))
    return gain


def normal_values(key, shape, width, limit, cuts=(), kind=jnp.bfloat16):
    drawn = jax.random.normal(key, shape, jnp.float32) * width
    if len(cuts) > 0:
        drawn = steps_of(key, shape, cuts, -0.22, 0.18) * drawn
    return jnp.clip(drawn, min=-limit, max=limit).astype(kind)


def setup_inputs(seed: int = 0) -> dict:
    arg_keys = jax.random.split(jax.random.key(seed), 10)
    alpha_fields = normal_values(arg_keys[0], (MEMBERS, NX, NY), 1.0, 6.0, ((0, 32), (1, 24)), jnp.float32)
    static_control = draw_static_control(jax.random.fold_in(arg_keys[9], 71), 0)
    perturbations = normal_values(arg_keys[2], (MEMBERS, NVAR, NX, NY), 1.0, 6.0, ((0, 32), (2, 24)))
    coef_table = jnp.clip(jax.random.uniform(arg_keys[3], (CLASSES,), jnp.float32, 0.12, 0.25), 0.12, 0.25)
    coef_class = with_ends(jax.random.randint(arg_keys[4], (NX, NY), 0, CLASSES), jax.random.fold_in(arg_keys[4], 1), 0, CLASSES - 1).astype(jnp.int32)
    obs_cells = with_ends(jax.random.randint(arg_keys[5], (TILES, OBS_TILE), 0, NVAR * CX * NY), jax.random.fold_in(arg_keys[5], 1), 0, (NVAR * CX * NY) - 1).astype(jnp.int32)
    obs_counts = draw_obs_counts(jax.random.fold_in(arg_keys[9], 71), 0)
    innovations = draw_innovations(jax.random.fold_in(arg_keys[9], 71), 0)
    obs_weights = jnp.clip(jnp.exp(math.log(100.0) - 2.3025851 * jax.random.uniform(arg_keys[8], (TILES, OBS_TILE), jnp.float32) ** steps_of(arg_keys[8], (TILES, OBS_TILE), ((0, 24),), -0.2, 0.2)), 10.0, 100.0)
    return dict(alpha_fields=alpha_fields, static_control=static_control, perturbations=perturbations, coef_table=coef_table, coef_class=coef_class, obs_cells=obs_cells, obs_counts=obs_counts, innovations=innovations, obs_weights=obs_weights)


def lookup(coef_table, classes):
    one_hot = (classes[None] == jnp.arange(coef_table.shape[0], dtype=jnp.int32)[:, None, None]).astype(jnp.float32)
    return jnp.sum(one_hot * coef_table[:, None, None], axis=0)


def beside_all(padded):
    return padded[:, 2:, 1:-1] + padded[:, :-2, 1:-1] + padded[:, 1:-1, 2:] + padded[:, 1:-1, :-2]


def pad_both(field):
    return jnp.pad(field, ((0, 0), (1, 1), (1, 1)))


def reference(alpha_fields, static_control, perturbations, coef_table, coef_class, obs_cells, obs_counts, innovations, obs_weights):
    kappa = lookup(coef_table, coef_class)
    fields = jnp.concatenate([alpha_fields, static_control], 0)
    current = fields
    for step in range(STEPS):
        current = current + kappa * (beside_all(pad_both(current)) - 4.0 * current)
    moved_alpha = current[:MEMBERS]
    moved_static = current[MEMBERS:]
    ens_scale = (MEMBERS - 1.0) ** -0.5

    def add_member(member, running):
        return running + perturbations[member].astype(jnp.float32) * moved_alpha[member][None]

    ensemble = lax.fori_loop(0, MEMBERS, add_member, jnp.zeros((NVAR, NX, NY), jnp.float32))
    increment = ens_scale * ensemble + moved_static
    by_strip = increment.reshape(NVAR, TILES, CX, NY).transpose(1, 0, 2, 3).reshape(TILES, NVAR * CX * NY)
    observed = jnp.take_along_axis(by_strip, obs_cells, 1)
    counted = jnp.arange(OBS_TILE, dtype=jnp.int32)[None] < obs_counts[:, None]
    residual = jnp.where(counted, (observed - innovations) * obs_weights, 0.0)

    def scatter_strip(cells, values):
        return jnp.zeros((NVAR * CX * NY,), jnp.float32).at[cells].add(values)

    strips = jax.vmap(scatter_strip)(obs_cells, residual)
    forcing = strips.reshape(TILES, NVAR, CX, NY).transpose(1, 0, 2, 3).reshape(NVAR, NX, NY)
    member_adj = lax.map(lambda pert_one: ens_scale * jnp.sum(pert_one.astype(jnp.float32) * forcing, 0), perturbations)
    current = jnp.concatenate([member_adj, forcing], 0)
    for step in range(STEPS):
        weighted = kappa * current
        current = current + (beside_all(pad_both(weighted)) - 4.0 * weighted)
    grads = fields + current
    return grads[:MEMBERS], grads[MEMBERS:]
```

```python
import functools

import jax
import jax.numpy as jnp
from jax import lax
from jax.experimental import pallas as pl
from jax.experimental.pallas import tpu as pltpu
from jax.sharding import PartitionSpec as P

MESH = pl.DeviceIdType.MESH
STEPS = 4
NVAR = 4
PAD = 8
LANES = 128
WIDE = 256


def beside_all(field):
    rows, cols = field.shape
    col = lax.broadcasted_iota(jnp.int32, field.shape, 1)
    above = pltpu.roll(field, 1, 0)
    below = pltpu.roll(field, rows - 1, 0)
    before = jnp.where(col == 0, 0.0, pltpu.roll(field, 1, 1))
    after = jnp.where(col == cols - 1, 0.0, pltpu.roll(field, cols - 1, 1))
    return above + below + before + after


def forward(field, kappa):
    for step in range(STEPS):
        field = field + kappa * (beside_all(field) - 4.0 * field)
    return field


def adjoint(field, kappa):
    for step in range(STEPS):
        weighted = kappa * field
        field = field + (beside_all(weighted) - 4.0 * weighted)
    return field


def kernel(
    tiles,
    members,
    alpha_hbm,
    static_hbm,
    pert_hbm,
    table_hbm,
    class_hbm,
    cells_hbm,
    counts_hbm,
    innov_hbm,
    weights_hbm,
    out_alpha,
    out_static,
    ext,
    kappa_ext,
    pert,
    classes,
    cells,
    innov,
    weights,
    table,
    counts,
    fwd_send,
    fwd_recv,
    static_send,
    static_recv,
    adj_send,
    adj_recv,
    inc,
    split,
    hot_lane,
    hot_row,
    obs,
    pair_buf,
    ring_buf,
    resid,
    adj,
    in_sem,
    fwd_sems,
    static_sems,
    adj_sems,
    pair_sems,
    ring_sems,
    swap_sems,
):
    owned, rows, cols = alpha_hbm.shape
    depth = members // 4
    slots = cells.shape[0]
    half = slots // 2
    scale = (owned * members - 1.0) ** (-0.5)
    m = lax.axis_index("mem")
    t = lax.axis_index("tile")
    core = lax.rem(m, 2)
    quad = lax.rem(m, 4)
    far = quad // 2
    level = m // 4
    stride = members // NVAR
    owner = lax.rem(m, stride) == 0
    var = m // stride
    has_up = t > 0
    has_down = t < tiles - 1

    core_mate = m + 1 - 2 * core
    far_mate = m + 2 - 4 * far
    both_mate = core_mate + 2 - 4 * far

    barrier = pltpu.get_barrier_semaphore()
    for mate in (core_mate, far_mate, both_mate):
        pl.semaphore_signal(barrier, inc=1, device_id={"mem": mate}, device_id_type=MESH)
    for d in range(1, depth):
        mate = lax.rem(level + d, depth) * 4 + quad
        pl.semaphore_signal(barrier, inc=1, device_id={"mem": mate}, device_id_type=MESH)

    @pl.when(has_up)
    def _():
        pl.semaphore_signal(barrier, inc=1, device_id={"tile": t - 1}, device_id_type=MESH)

    @pl.when(has_down)
    def _():
        pl.semaphore_signal(barrier, inc=1, device_id={"tile": t + 1}, device_id_type=MESH)

    own = pl.ds(PAD, rows)
    loads = [
        pltpu.make_async_copy(class_hbm, classes, in_sem.at[0]),
        pltpu.make_async_copy(table_hbm, table, in_sem.at[1]),
        pltpu.make_async_copy(alpha_hbm, ext.at[pl.ds(0, owned), own], in_sem.at[2]),
        pltpu.make_async_copy(static_hbm.at[var], ext.at[owned, own], in_sem.at[3]),
        pltpu.make_async_copy(cells_hbm, cells, in_sem.at[4]),
        pltpu.make_async_copy(counts_hbm, counts, in_sem.at[5]),
        pltpu.make_async_copy(innov_hbm, innov, in_sem.at[6]),
        pltpu.make_async_copy(weights_hbm, weights, in_sem.at[7]),
        pltpu.make_async_copy(pert_hbm, pert, in_sem.at[8]),
    ]
    for load in loads:
        load.start()

    for edge, missing in ((0, t == 0), (1, t == tiles - 1)):

        @pl.when(missing)
        def _():
            fwd_recv[edge] = jnp.zeros(fwd_recv.shape[1:], jnp.float32)
            static_recv[edge] = jnp.zeros(static_recv.shape[1:], jnp.float32)
            adj_recv[edge] = jnp.zeros(adj_recv.shape[1:], jnp.float32)

    def exchange(send, recv, sems):
        up = pltpu.make_async_remote_copy(
            send.at[0], recv.at[1], sems.at[0, 0], sems.at[1, 1], device_id={"tile": t - 1}, device_id_type=MESH
        )
        down = pltpu.make_async_remote_copy(
            send.at[1], recv.at[0], sems.at[0, 1], sems.at[1, 0], device_id={"tile": t + 1}, device_id_type=MESH
        )
        return up, down

    def start(pair):
        @pl.when(has_up)
        def _():
            pair[0].start()

        @pl.when(has_down)
        def _():
            pair[1].start()

    def wait(pair):
        @pl.when(has_up)
        def _():
            pair[0].wait_send()
            pair[1].wait_recv()

        @pl.when(has_down)
        def _():
            pair[1].wait_send()
            pair[0].wait_recv()

    loads[0].wait()
    loads[1].wait()
    kind = classes[...]
    kappa = jnp.full(kind.shape, table[0], jnp.float32)
    for i in range(1, table.shape[0]):
        kappa = jnp.where(kind == i, table[i], kappa)
    kappa_ext[own] = kappa
    fwd_send[0, pl.ds(4 * owned, STEPS)] = kappa[:STEPS]
    fwd_send[1, pl.ds(4 * owned, STEPS)] = kappa[rows - STEPS :]
    loads[2].wait()
    for f in range(owned):
        fwd_send[0, pl.ds(4 * f, STEPS)] = ext[f, pl.ds(PAD, STEPS)]
        fwd_send[1, pl.ds(4 * f, STEPS)] = ext[f, pl.ds(PAD + rows - STEPS, STEPS)]
    loads[3].wait()
    static_send[0] = ext[owned, pl.ds(PAD, STEPS)]
    static_send[1] = ext[owned, pl.ds(PAD + rows - STEPS, STEPS)]

    pl.semaphore_wait(barrier, depth + 2 + has_up.astype(jnp.int32) + has_down.astype(jnp.int32))
    fwd_pair = exchange(fwd_send, fwd_recv, fwd_sems)
    start(fwd_pair)
    static_pair = exchange(static_send, static_recv, static_sems)

    @pl.when(owner)
    def _():
        start(static_pair)

    loads[4].wait()
    folds = cols // WIDE
    field_rows = NVAR * rows
    lane_of = lax.broadcasted_iota(jnp.int32, (WIDE, LANES), 0)
    row_of = lax.broadcasted_iota(jnp.int32, (folds * field_rows, LANES), 0)
    row_of = lax.rem(row_of, field_rows) * folds + row_of // field_rows

    def make_hot(i, carry):
        at = pl.ds(pl.multiple_of(i * LANES, LANES), LANES)
        cell = cells[pl.ds(i, 1), :]
        hot_lane[:, at] = jnp.where(lane_of == lax.rem(cell, WIDE), 1.0, 0.0).astype(jnp.bfloat16)
        hot_row[:, at] = jnp.where(row_of == cell // WIDE, 1.0, 0.0).astype(jnp.bfloat16)
        return carry

    lax.fori_loop(0, slots, make_hot, 0)
    for load in loads[5:]:
        load.wait()

    wait(fwd_pair)

    def with_rows(ref, f, above, below):
        blank = jnp.zeros((PAD - STEPS, cols), jnp.float32)
        ref[f, pl.ds(0, PAD)] = jnp.concatenate([blank, above], 0)
        ref[f, pl.ds(PAD + rows, PAD)] = jnp.concatenate([below, blank], 0)

    blank = jnp.zeros((PAD - STEPS, cols), jnp.float32)
    kappa_ext[pl.ds(0, PAD)] = jnp.concatenate([blank, fwd_recv[0, pl.ds(4 * owned, STEPS)]], 0)
    kappa_ext[pl.ds(PAD + rows, PAD)] = jnp.concatenate([fwd_recv[1, pl.ds(4 * owned, STEPS)], blank], 0)
    for f in range(owned):
        with_rows(ext, f, fwd_recv[0, pl.ds(4 * f, STEPS)], fwd_recv[1, pl.ds(4 * f, STEPS)])

    inc[...] = jnp.zeros(inc.shape, jnp.float32)

    def move(f, carry):
        moved = forward(ext[f], kappa_ext[...])[PAD : PAD + rows] * scale
        for v in range(NVAR):
            inc[v] = inc[v] + pert[f, v].astype(jnp.float32) * moved
        return carry

    lax.fori_loop(0, owned, move, 0)

    @pl.when(owner)
    def _():
        wait(static_pair)
        with_rows(ext, owned, static_recv[0], static_recv[1])
        inc[var] = inc[var] + forward(ext[owned], kappa_ext[...])[PAD : PAD + rows]

    for fold in range(folds):
        part = inc[:, :, pl.ds(fold * WIDE, WIDE)].reshape(field_rows, WIDE)
        high = part.astype(jnp.bfloat16)
        low = (part - high.astype(jnp.float32)).astype(jnp.bfloat16)
        split[0, pl.ds(fold * field_rows, field_rows)] = high
        split[1, pl.ds(fold * field_rows, field_rows)] = low

    row_wide = lax.broadcasted_iota(jnp.int32, (folds * field_rows, WIDE), 0)
    row_wide = lax.rem(row_wide, field_rows) * folds + row_wide // field_rows

    def pick(i, carry):
        at = pl.ds(pl.multiple_of(i * WIDE, WIDE), WIDE)
        hot = hot_lane[:, at]
        found = jnp.dot(split[0], hot, preferred_element_type=jnp.float32)
        found = found + jnp.dot(split[1], hot, preferred_element_type=jnp.float32)
        cell = jnp.concatenate([cells[pl.ds(2 * i, 1), :], cells[pl.ds(2 * i + 1, 1), :]], 1)
        value = jnp.sum(jnp.where(row_wide == cell // WIDE, found, 0.0), 0, keepdims=True)
        obs[pl.ds(2 * i, 1), :] = value[:, :LANES]
        obs[pl.ds(2 * i + 1, 1), :] = value[:, LANES:]
        return carry

    mine = pl.ds(pl.multiple_of(core * half, 8), half)
    others = pl.ds(pl.multiple_of((1 - core) * half, 8), half)
    blocks = half // 2

    def pair_copy(source, mate, sender, at):
        return pltpu.make_async_remote_copy(
            source, pair_buf.at[sender], pair_sems.at[0, at], pair_sems.at[1, sender], device_id={"mem": mate}, device_id_type=MESH
        )

    lax.fori_loop((1 - core) * blocks, (2 - core) * blocks, pick, 0)
    pair_core = pair_copy(obs.at[others], core_mate, quad, 0)
    pair_both = pair_copy(obs.at[others], both_mate, quad, 1)
    pair_core.start()
    pair_both.start()
    lax.fori_loop(core * blocks, (core + 1) * blocks, pick, 0)
    pair_far = pair_copy(obs.at[mine], far_mate, quad, 2)
    pair_far.start()
    pair_buf[quad] = obs[mine]
    for mate in (core_mate, far_mate, both_mate):
        pair_copy(obs.at[mine], mate, lax.rem(mate, 4), 0).wait_recv()
    ring_buf[level] = pair_buf[0] + pair_buf[1] + pair_buf[2] + pair_buf[3]

    def ring_copy(d):
        to = lax.rem(level + d, depth) * 4 + quad
        return pltpu.make_async_remote_copy(
            ring_buf.at[level], ring_buf.at[level], ring_sems.at[0, d], ring_sems.at[1, level], device_id={"mem": to}, device_id_type=MESH
        )

    for d in range(1, depth):
        ring_copy(d).start()
    for d in range(1, depth):
        other = lax.rem(level + d, depth)
        pltpu.make_async_remote_copy(
            ring_buf.at[other],
            ring_buf.at[other],
            ring_sems.at[0, d],
            ring_sems.at[1, other],
            device_id={"mem": other * 4 + quad},
            device_id_type=MESH,
        ).wait_recv()
    observed = ring_buf[0]
    for d in range(1, depth):
        observed = observed + ring_buf[d]
    slot = lax.broadcasted_iota(jnp.int32, (half, LANES), 0) * LANES + lax.broadcasted_iota(jnp.int32, (half, LANES), 1)
    slot = slot + core * (half * LANES)
    resid[mine] = jnp.where(slot < counts[0], (observed - innov[mine]) * weights[mine], 0.0)
    swap = pltpu.make_async_remote_copy(
        resid.at[mine], resid.at[mine], swap_sems.at[0], swap_sems.at[1], device_id={"mem": core_mate}, device_id_type=MESH
    )
    swap.start()

    def spread(first):
        def add(i, total):
            at = pl.ds(pl.multiple_of((first + i) * WIDE, WIDE), WIDE)
            value = jnp.concatenate([resid[pl.ds(2 * (first + i), 1), :], resid[pl.ds(2 * (first + i) + 1, 1), :]], 1)
            high = value.astype(jnp.bfloat16)
            low = (value - high.astype(jnp.float32)).astype(jnp.bfloat16)
            hot = hot_lane[:, at]
            both = jnp.concatenate([hot * high, hot * low], 1)
            rows_hot = hot_row[:, at]
            return total + lax.dot_general(
                jnp.concatenate([rows_hot, rows_hot], 1), both, (((1,), (1,)), ((), ())), preferred_element_type=jnp.float32
            )

        return lax.fori_loop(0, blocks, add, jnp.zeros((folds * field_rows, WIDE), jnp.float32))

    first_part = spread(core * blocks)
    swap.wait()
    forcing = first_part + spread((1 - core) * blocks)
    for fold in range(folds):
        part = forcing[fold * field_rows : (fold + 1) * field_rows]
        adj[pl.ds(owned, NVAR), own, pl.ds(fold * WIDE, WIDE)] = part.reshape(NVAR, rows, WIDE)

    def weigh(f, carry):
        total = pert[f, 0].astype(jnp.float32) * adj[owned, own]
        for v in range(1, NVAR):
            total = total + pert[f, v].astype(jnp.float32) * adj[owned + v, own]
        adj[f, own] = scale * total
        return carry

    lax.fori_loop(0, owned, weigh, 0)
    for f in range(owned + NVAR):
        adj_send[0, pl.ds(4 * f, STEPS)] = adj[f, pl.ds(PAD, STEPS)]
        adj_send[1, pl.ds(4 * f, STEPS)] = adj[f, pl.ds(PAD + rows - STEPS, STEPS)]
    adj_pair = exchange(adj_send, adj_recv, adj_sems)
    start(adj_pair)
    pair_core.wait_send()
    pair_both.wait_send()
    pair_far.wait_send()
    for d in range(1, depth):
        ring_copy(d).wait_send()
    wait(adj_pair)
    for f in range(owned + NVAR):
        with_rows(adj, f, adj_recv[0, pl.ds(4 * f, STEPS)], adj_recv[1, pl.ds(4 * f, STEPS)])

    def finish_alpha(f, carry):
        out_alpha[f] = adjoint(adj[f], kappa_ext[...])[PAD : PAD + rows]
        return carry

    def finish_static(v, carry):
        out_static[v] = adjoint(adj[owned + v], kappa_ext[...])[PAD : PAD + rows]
        return carry

    lax.fori_loop(0, owned, finish_alpha, 0)
    lax.fori_loop(0, NVAR, finish_static, 0)


def body(tiles, members, alpha_fields, static_control, perturbations, coef_table, coef_class, obs_cells, obs_counts, innovations, obs_weights):
    owned, rows, cols = alpha_fields.shape
    slots = obs_cells.shape[1] // LANES
    folded = (slots, LANES)
    half = slots // 2
    depth = members // 4
    fields = owned + NVAR
    packed = 4 * (owned + 1)
    adj_packed = -(-4 * fields // 8) * 8
    deep = rows + 2 * PAD
    field_rows = cols // WIDE * NVAR * rows
    f32, bf16, i32 = jnp.float32, jnp.bfloat16, jnp.int32
    anywhere = pl.BlockSpec(memory_space=pl.ANY)
    in_vmem = pl.BlockSpec(memory_space=pltpu.VMEM)
    dma = pltpu.SemaphoreType.DMA
    moved = pl.pallas_call(
        functools.partial(kernel, tiles, members),
        out_shape=(jax.ShapeDtypeStruct((owned, rows, cols), f32), jax.ShapeDtypeStruct((NVAR, rows, cols), f32)),
        in_specs=[anywhere] * 9,
        out_specs=(in_vmem, in_vmem),
        scratch_shapes=[
            pltpu.VMEM((owned + 1, deep, cols), f32),
            pltpu.VMEM((deep, cols), f32),
            pltpu.VMEM((owned, NVAR, rows, cols), bf16),
            pltpu.VMEM((rows, cols), i32),
            pltpu.VMEM(folded, i32),
            pltpu.VMEM(folded, f32),
            pltpu.VMEM(folded, f32),
            pltpu.SMEM(coef_table.shape, f32),
            pltpu.SMEM(obs_counts.shape, i32),
            pltpu.VMEM((2, packed, cols), f32),
            pltpu.VMEM((2, packed, cols), f32),
            pltpu.VMEM((2, STEPS, cols), f32),
            pltpu.VMEM((2, STEPS, cols), f32),
            pltpu.VMEM((2, adj_packed, cols), f32),
            pltpu.VMEM((2, adj_packed, cols), f32),
            pltpu.VMEM((NVAR, rows, cols), f32),
            pltpu.VMEM((2, field_rows, WIDE), bf16),
            pltpu.VMEM((WIDE, slots * LANES), bf16),
            pltpu.VMEM((field_rows, slots * LANES), bf16),
            pltpu.VMEM(folded, f32),
            pltpu.VMEM((4, half, LANES), f32),
            pltpu.VMEM((depth, half, LANES), f32),
            pltpu.VMEM(folded, f32),
            pltpu.VMEM((fields, deep, cols), f32),
            dma((9,)),
            dma((2, 2)),
            dma((2, 2)),
            dma((2, 2)),
            dma((2, 4)),
            dma((2, depth)),
            dma((2,)),
        ],
        compiler_params=pltpu.CompilerParams(collective_id=0, has_side_effects=True),
    )(
        alpha_fields,
        static_control,
        perturbations,
        coef_table,
        coef_class,
        obs_cells.reshape(folded),
        obs_counts,
        innovations.reshape(folded),
        obs_weights.reshape(folded),
    )
    return alpha_fields + moved[0], static_control + moved[1]


def solution(mesh):
    in_specs = (
        P("mem", "tile", None),
        P(None, "tile", None),
        P("mem", None, "tile", None),
        P(),
        P("tile", None),
        P("tile", None),
        P("tile"),
        P("tile", None),
        P("tile", None),
    )
    out_specs = (P("mem", "tile", None), P(None, "tile", None))
    run = functools.partial(body, mesh.shape["tile"], mesh.shape["mem"])
    return jax.shard_map(run, mesh=mesh, in_specs=in_specs, out_specs=out_specs, check_vma=False)
```

```python
import functools

import jax
import jax.numpy as jnp
from jax import lax
from jax.experimental import pallas as pl
from jax.experimental.pallas import tpu as pltpu
from jax.sharding import PartitionSpec as P

MESH = pl.DeviceIdType.MESH
STEPS = 4
NVAR = 4
PAD = 8
LANES = 128
WIDE = 256
CHUNK = 1024


def advance(source, target, kappa, keep, f, starts):
    tiles = source.shape[1]
    lane = lax.broadcasted_iota(jnp.int32, (8, LANES), 1)
    first, last = lane == 0, lane == LANES - 1
    for r in starts:
        here = [source[f, j, pl.ds(r, 8), :] for j in range(tiles)]
        right = [pltpu.roll(a, 1, 1) for a in here]
        left = [pltpu.roll(a, LANES - 1, 1) for a in here]
        for j in range(tiles):
            before = jnp.where(first, right[j - 1] if j else 0.0, right[j])
            after = jnp.where(last, left[j + 1] if j < tiles - 1 else 0.0, left[j])
            around = (source[f, j, pl.ds(r - 1, 8), :] + source[f, j, pl.ds(r + 1, 8), :]) + (before + after)
            target[f, j, pl.ds(r, 8), :] = keep[j, pl.ds(r, 8), :] * here[j] + kappa[j, pl.ds(r, 8), :] * around


def inner_rows(stages, kappa, keep, f, rows):
    for s in range(STEPS):
        advance(stages[s], stages[s + 1], kappa, keep, f, range(PAD, PAD + rows, 8))


def border_rows(stages, kappa, keep, fields, rows):
    for s in range(STEPS):
        for f in fields:
            advance(stages[s], stages[s + 1], kappa, keep, f, (PAD - STEPS + s, PAD + rows - STEPS - s))


def kernel(
    tiles,
    members,
    alpha_hbm,
    static_hbm,
    pert_hbm,
    table_hbm,
    class_hbm,
    cells_hbm,
    counts_hbm,
    innov_hbm,
    weights_hbm,
    out_alpha,
    out_static,
    alpha,
    static,
    pert,
    classes,
    cells,
    innov,
    weights,
    table,
    counts,
    kappa,
    keep,
    inverse,
    fwd0,
    fwd1,
    fwd2,
    fwd3,
    fwd4,
    adj0,
    adj1,
    adj2,
    adj3,
    adj4,
    fwd_send,
    fwd_recv,
    static_send,
    static_recv,
    adj_send,
    adj_recv,
    field,
    split,
    hot_lane,
    hot_row,
    obs,
    pair_buf,
    ring_buf,
    resid,
    in_sem,
    fwd_sems,
    static_sems,
    adj_sems,
    pair_sems,
    ring_sems,
    swap_sems,
):
    owned, rows, cols = alpha.shape
    lane_tiles = cols // LANES
    folds = cols // WIDE
    field_rows = NVAR * rows
    depth = members // 4
    slots = cells.shape[0]
    half = slots // 2
    scale = (owned * members - 1.0) ** (-0.5)
    fwd = (fwd0, fwd1, fwd2, fwd3, fwd4)
    adj = (adj0, adj1, adj2, adj3, adj4)
    m = lax.axis_index("mem")
    t = lax.axis_index("tile")
    core = lax.rem(m, 2)
    quad = lax.rem(m, 4)
    far = quad // 2
    level = m // 4
    stride = members // NVAR
    owner = lax.rem(m, stride) == stride // 2
    var = m // stride
    has_up = t > 0
    has_down = t < tiles - 1

    core_mate = m + 1 - 2 * core
    far_mate = m + 2 - 4 * far
    both_mate = core_mate + 2 - 4 * far

    barrier = pltpu.get_barrier_semaphore()

    @pl.when(has_up)
    def _():
        pl.semaphore_signal(barrier, inc=1, device_id={"tile": t - 1}, device_id_type=MESH)

    @pl.when(has_down)
    def _():
        pl.semaphore_signal(barrier, inc=1, device_id={"tile": t + 1}, device_id_type=MESH)

    for mate in (core_mate, far_mate, both_mate):
        pl.semaphore_signal(barrier, inc=1, device_id={"mem": mate}, device_id_type=MESH)
    for d in range(1, depth):
        mate = lax.rem(level + d, depth) * 4 + quad
        pl.semaphore_signal(barrier, inc=1, device_id={"mem": mate}, device_id_type=MESH)

    loads = [
        pltpu.make_async_copy(class_hbm, classes, in_sem.at[0]),
        pltpu.make_async_copy(table_hbm, table, in_sem.at[1]),
        pltpu.make_async_copy(alpha_hbm, alpha, in_sem.at[2]),
        pltpu.make_async_copy(static_hbm, static, in_sem.at[3]),
        pltpu.make_async_copy(cells_hbm, cells, in_sem.at[4]),
        pltpu.make_async_copy(counts_hbm, counts, in_sem.at[5]),
        pltpu.make_async_copy(innov_hbm, innov, in_sem.at[6]),
        pltpu.make_async_copy(weights_hbm, weights, in_sem.at[7]),
        pltpu.make_async_copy(pert_hbm, pert, in_sem.at[8]),
    ]
    for load in loads:
        load.start()

    for edge, missing in ((0, t == 0), (1, t == tiles - 1)):

        @pl.when(missing)
        def _():
            fwd_recv[edge] = jnp.zeros(fwd_recv.shape[1:], jnp.float32)
            static_recv[edge] = jnp.zeros(static_recv.shape[1:], jnp.float32)
            adj_recv[edge] = jnp.zeros(adj_recv.shape[1:], jnp.float32)

    def exchange(send, recv, sems):
        up = pltpu.make_async_remote_copy(
            send.at[0], recv.at[1], sems.at[0, 0], sems.at[1, 1], device_id={"tile": t - 1}, device_id_type=MESH
        )
        down = pltpu.make_async_remote_copy(
            send.at[1], recv.at[0], sems.at[0, 1], sems.at[1, 0], device_id={"tile": t + 1}, device_id_type=MESH
        )
        return up, down

    def start(pair):
        @pl.when(has_up)
        def _():
            pair[0].start()

        @pl.when(has_down)
        def _():
            pair[1].start()

    def wait(pair):
        @pl.when(has_up)
        def _():
            pair[0].wait_send()
            pair[1].wait_recv()

        @pl.when(has_down)
        def _():
            pair[1].wait_send()
            pair[0].wait_recv()

    def pack(send, g, top, bottom):
        at = pl.ds(4 * (g % 2), STEPS)
        send[0, g // 2, at, :] = top
        send[1, g // 2, at, :] = bottom

    def unpack(recv, g, target, index):
        at = pl.ds(4 * (g % 2), STEPS)
        target[(*index, pl.ds(PAD - STEPS, STEPS), slice(None))] = recv[0, g // 2, at, :]
        target[(*index, pl.ds(PAD + rows, STEPS), slice(None))] = recv[1, g // 2, at, :]

    own = pl.ds(PAD, rows)
    top_rows = pl.ds(PAD, STEPS)
    bottom_rows = pl.ds(PAD + rows - STEPS, STEPS)
    columns = [pl.ds(j * LANES, LANES) for j in range(lane_tiles)]

    loads[0].wait()
    loads[1].wait()
    for j in range(lane_tiles):
        kind = classes[:, columns[j]]
        value = jnp.full(kind.shape, table[0], jnp.float32)
        for i in range(1, table.shape[0]):
            value = jnp.where(kind == i, table[i], value)
        kappa[j, own, :] = value
        keep[j, own, :] = 1.0 - 4.0 * value
        pack(fwd_send, owned * lane_tiles + j, value[:STEPS], value[rows - STEPS :])
    loads[2].wait()
    for f in range(owned):
        for j in range(lane_tiles):
            fwd0[f, j, own, :] = alpha[f, :, columns[j]]
            pack(fwd_send, f * lane_tiles + j, fwd0[f, j, top_rows, :], fwd0[f, j, bottom_rows, :])
    loads[3].wait()

    @pl.when(owner)
    def _():
        for j in range(lane_tiles):
            fwd0[owned, j, own, :] = static[var, :, columns[j]]
            pack(static_send, j, fwd0[owned, j, top_rows, :], fwd0[owned, j, bottom_rows, :])

    pl.semaphore_wait(barrier, depth + 2 + has_up.astype(jnp.int32) + has_down.astype(jnp.int32))
    fwd_pair = exchange(fwd_send, fwd_recv, fwd_sems)
    start(fwd_pair)
    static_pair = exchange(static_send, static_recv, static_sems)

    @pl.when(owner)
    def _():
        start(static_pair)

    loads[4].wait()
    lane_of = lax.broadcasted_iota(jnp.int32, (WIDE, LANES), 0)
    three_rows = folds * lax.broadcasted_iota(jnp.int32, (field_rows, LANES), 0)

    def make_hot_lane(i, carry):
        at = pl.ds(pl.multiple_of(i * LANES, LANES), LANES)
        hot_lane[:, at] = jnp.where(lane_of == (cells[pl.ds(i, 1), :] & (WIDE - 1)), 1.0, 0.0).astype(jnp.bfloat16)
        return carry

    def make_hot_row(i, carry):
        at = pl.ds(pl.multiple_of(i * LANES, LANES), LANES)
        row = cells[pl.ds(i, 1), :] // WIDE
        for fold in range(folds):
            hot = jnp.where(three_rows == row - fold, 1.0, 0.0).astype(jnp.bfloat16)
            hot_row[pl.ds(fold * field_rows, field_rows), at] = hot
        return carry

    lax.fori_loop(0, slots, make_hot_lane, 0)

    def inner_fwd(f, carry):
        inner_rows(fwd, kappa, keep, f, rows)
        return carry

    lax.fori_loop(0, owned, inner_fwd, 0)

    @pl.when(owner)
    def _():
        inner_rows(fwd, kappa, keep, owned, rows)

    for load in loads[5:]:
        load.wait()

    wait(fwd_pair)
    for j in range(lane_tiles):
        unpack(fwd_recv, owned * lane_tiles + j, kappa, (j,))
        for at in (pl.ds(PAD - STEPS, STEPS), pl.ds(PAD + rows, STEPS)):
            keep[j, at, :] = 1.0 - 4.0 * kappa[j, at, :]
        for f in range(owned):
            unpack(fwd_recv, f * lane_tiles + j, fwd0, (f, j))
    border_rows(fwd, kappa, keep, range(owned), rows)

    def place(v, j):
        return pl.ds((j * LANES // WIDE) * field_rows + v * rows, rows), pl.ds(j * LANES % WIDE, LANES)

    for j in range(lane_tiles):
        for v in range(NVAR):
            total = pert[0, v, :, columns[j]].astype(jnp.float32) * fwd4[0, j, own, :]
            for f in range(1, owned):
                total = total + pert[f, v, :, columns[j]].astype(jnp.float32) * fwd4[f, j, own, :]
            field[place(v, j)] = scale * total

    @pl.when(owner)
    def _():
        wait(static_pair)
        for j in range(lane_tiles):
            unpack(static_recv, j, fwd0, (owned, j))
        border_rows(fwd, kappa, keep, (owned,), rows)
        for j in range(lane_tiles):
            at = place(0, j)
            at = (pl.ds(pl.multiple_of(at[0].start + var * rows, rows), rows), at[1])
            field[at] = field[at] + fwd4[owned, j, own, :]

    high = field[...].astype(jnp.bfloat16)
    split[0] = high
    split[1] = (field[...] - high.astype(jnp.float32)).astype(jnp.bfloat16)

    per_chunk = CHUNK // LANES
    row_chunk = folds * lax.broadcasted_iota(jnp.int32, (field_rows, CHUNK), 0)

    def pick(i, carry):
        at = pl.ds(pl.multiple_of(i * CHUNK, CHUNK), CHUNK)
        hot = hot_lane[:, at]
        found = jnp.dot(split[0], hot, preferred_element_type=jnp.float32)
        found = found + jnp.dot(split[1], hot, preferred_element_type=jnp.float32)
        row = jnp.concatenate([cells[pl.ds(per_chunk * i + q, 1), :] for q in range(per_chunk)], 1) // WIDE
        kept = jnp.zeros((field_rows, CHUNK), jnp.float32)
        for fold in range(folds):
            kept = jnp.where(row_chunk == row - fold, found[fold * field_rows : (fold + 1) * field_rows], kept)
        value = jnp.sum(kept, 0, keepdims=True)
        for q in range(per_chunk):
            obs[pl.ds(per_chunk * i + q, 1), :] = value[:, q * LANES : (q + 1) * LANES]
        return carry

    mine = pl.ds(pl.multiple_of(core * half, 8), half)
    others = pl.ds(pl.multiple_of((1 - core) * half, 8), half)
    blocks = half // per_chunk

    def pair_copy(source, mate, sender, at):
        return pltpu.make_async_remote_copy(
            source, pair_buf.at[sender], pair_sems.at[0, at], pair_sems.at[1, sender], device_id={"mem": mate}, device_id_type=MESH
        )

    lax.fori_loop((1 - core) * blocks, (2 - core) * blocks, pick, 0)
    pair_both = pair_copy(obs.at[others], both_mate, quad, 1)
    pair_core = pair_copy(obs.at[others], core_mate, quad, 0)
    pair_both.start()
    pair_core.start()
    lax.fori_loop(core * blocks, (core + 1) * blocks, pick, 0)
    pair_far = pair_copy(obs.at[mine], far_mate, quad, 2)
    pair_far.start()
    pair_buf[quad] = obs[mine]
    lax.fori_loop(0, slots, make_hot_row, 0)
    for mate in (core_mate, far_mate, both_mate):
        pair_copy(obs.at[mine], mate, lax.rem(mate, 4), 0).wait_recv()
    ring_buf[level] = pair_buf[0] + pair_buf[1] + pair_buf[2] + pair_buf[3]

    def ring_copy(d):
        to = lax.rem(level + d, depth) * 4 + quad
        return pltpu.make_async_remote_copy(
            ring_buf.at[level], ring_buf.at[level], ring_sems.at[0, d], ring_sems.at[1, level], device_id={"mem": to}, device_id_type=MESH
        )

    order = sorted(range(1, depth), key=lambda d: -min(d, depth - d))
    for d in order:
        ring_copy(d).start()
    for j in range(lane_tiles):
        inverse[j] = 1.0 / kappa[j, own, :]
    for d in range(1, depth):
        other = lax.rem(level + d, depth)
        pltpu.make_async_remote_copy(
            ring_buf.at[other],
            ring_buf.at[other],
            ring_sems.at[0, d],
            ring_sems.at[1, other],
            device_id={"mem": other * 4 + quad},
            device_id_type=MESH,
        ).wait_recv()
    observed = ring_buf[0]
    for d in range(1, depth):
        observed = observed + ring_buf[d]
    slot = lax.broadcasted_iota(jnp.int32, (half, LANES), 0) * LANES + lax.broadcasted_iota(jnp.int32, (half, LANES), 1)
    slot = slot + core * (half * LANES)
    resid[mine] = jnp.where(slot < counts[0], (observed - innov[mine]) * weights[mine], 0.0)
    swap = pltpu.make_async_remote_copy(
        resid.at[mine], resid.at[mine], swap_sems.at[0], swap_sems.at[1], device_id={"mem": core_mate}, device_id_type=MESH
    )
    swap.start()

    def spread(which):
        at = pl.ds(pl.multiple_of(which * (half * LANES), half * LANES), half * LANES)
        value = jnp.concatenate([resid[pl.ds(which * half + q, 1), :] for q in range(half)], 1)
        high = value.astype(jnp.bfloat16)
        low = (value - high.astype(jnp.float32)).astype(jnp.bfloat16)
        hot = hot_lane[:, at]
        row = hot_row[:, at]
        return lax.dot_general(
            jnp.concatenate([row, row], 1),
            jnp.concatenate([hot * high, hot * low], 1),
            (((1,), (1,)), ((), ())),
            preferred_element_type=jnp.float32,
        )

    field[...] = spread(core)
    swap.wait()
    field[...] = field[...] + spread(1 - core)

    for j in range(lane_tiles):
        forcing = [field[place(v, j)] for v in range(NVAR)]
        factor = kappa[j, own, :]
        for v in range(NVAR):
            adj0[owned + v, j, own, :] = factor * forcing[v]
        for f in range(owned):
            total = pert[f, 0, :, columns[j]].astype(jnp.float32) * forcing[0]
            for v in range(1, NVAR):
                total = total + pert[f, v, :, columns[j]].astype(jnp.float32) * forcing[v]
            adj0[f, j, own, :] = factor * (scale * total)
        for f in range(owned + NVAR):
            pack(adj_send, f * lane_tiles + j, adj0[f, j, top_rows, :], adj0[f, j, bottom_rows, :])
    adj_pair = exchange(adj_send, adj_recv, adj_sems)
    start(adj_pair)

    def inner_adj(f, carry):
        inner_rows(adj, kappa, keep, f, rows)
        return carry

    lax.fori_loop(0, owned + NVAR, inner_adj, 0)
    pair_core.wait_send()
    pair_both.wait_send()
    pair_far.wait_send()
    for d in range(1, depth):
        ring_copy(d).wait_send()
    wait(adj_pair)
    for j in range(lane_tiles):
        for f in range(owned + NVAR):
            unpack(adj_recv, f * lane_tiles + j, adj0, (f, j))
    border_rows(adj, kappa, keep, range(owned + NVAR), rows)
    for j in range(lane_tiles):
        for f in range(owned):
            out_alpha[f, :, columns[j]] = alpha[f, :, columns[j]] + adj4[f, j, own, :] * inverse[j]
        for v in range(NVAR):
            out_static[v, :, columns[j]] = static[v, :, columns[j]] + adj4[owned + v, j, own, :] * inverse[j]


def body(tiles, members, alpha_fields, static_control, perturbations, coef_table, coef_class, obs_cells, obs_counts, innovations, obs_weights):
    owned, rows, cols = alpha_fields.shape
    slots = obs_cells.shape[1] // LANES
    folded = (slots, LANES)
    half = slots // 2
    depth = members // 4
    fields = owned + NVAR
    lane_tiles = cols // LANES
    deep = rows + 2 * PAD
    field_rows = cols // WIDE * NVAR * rows
    f32, bf16, i32 = jnp.float32, jnp.bfloat16, jnp.int32
    anywhere = pl.BlockSpec(memory_space=pl.ANY)
    in_hbm = functools.partial(pltpu.with_memory_space_constraint, memory_space=pltpu.HBM)
    in_vmem = pl.BlockSpec(memory_space=pltpu.VMEM)
    dma = pltpu.SemaphoreType.DMA

    def message(count):
        return [pltpu.VMEM((2, count * lane_tiles // 2, 8, LANES), f32)] * 2

    return pl.pallas_call(
        functools.partial(kernel, tiles, members),
        out_shape=(jax.ShapeDtypeStruct((owned, rows, cols), f32), jax.ShapeDtypeStruct((NVAR, rows, cols), f32)),
        in_specs=[anywhere] * 9,
        out_specs=(in_vmem, in_vmem),
        scratch_shapes=[
            pltpu.VMEM((owned, rows, cols), f32),
            pltpu.VMEM((NVAR, rows, cols), f32),
            pltpu.VMEM((owned, NVAR, rows, cols), bf16),
            pltpu.VMEM((rows, cols), i32),
            pltpu.VMEM(folded, i32),
            pltpu.VMEM(folded, f32),
            pltpu.VMEM(folded, f32),
            pltpu.SMEM(coef_table.shape, f32),
            pltpu.SMEM(obs_counts.shape, i32),
            pltpu.VMEM((lane_tiles, deep, LANES), f32),
            pltpu.VMEM((lane_tiles, deep, LANES), f32),
            pltpu.VMEM((lane_tiles, rows, LANES), f32),
            *[pltpu.VMEM((owned + 1, lane_tiles, deep, LANES), f32)] * (STEPS + 1),
            *[pltpu.VMEM((fields, lane_tiles, deep, LANES), f32)] * (STEPS + 1),
            *message(owned + 1),
            *message(1),
            *message(fields),
            pltpu.VMEM((field_rows, WIDE), f32),
            pltpu.VMEM((2, field_rows, WIDE), bf16),
            pltpu.VMEM((WIDE, slots * LANES), bf16),
            pltpu.VMEM((field_rows, slots * LANES), bf16),
            pltpu.VMEM(folded, f32),
            pltpu.VMEM((4, half, LANES), f32),
            pltpu.VMEM((depth, half, LANES), f32),
            pltpu.VMEM(folded, f32),
            dma((9,)),
            dma((2, 2)),
            dma((2, 2)),
            dma((2, 2)),
            dma((2, 4)),
            dma((2, depth)),
            dma((2,)),
        ],
        compiler_params=pltpu.CompilerParams(collective_id=0, has_side_effects=True, vmem_limit_bytes=48 * 2**20),
    )(
        in_hbm(alpha_fields),
        in_hbm(static_control),
        in_hbm(perturbations),
        in_hbm(coef_table),
        in_hbm(coef_class),
        in_hbm(obs_cells.reshape(folded)),
        obs_counts,
        in_hbm(innovations.reshape(folded)),
        in_hbm(obs_weights.reshape(folded)),
    )


def solution(mesh):
    in_specs = (
        P("mem", "tile", None),
        P(None, "tile", None),
        P("mem", None, "tile", None),
        P(),
        P("tile", None),
        P("tile", None),
        P("tile"),
        P("tile", None),
        P("tile", None),
    )
    out_specs = (P("mem", "tile", None), P(None, "tile", None))
    run = functools.partial(body, mesh.shape["tile"], mesh.shape["mem"])
    return jax.shard_map(run, mesh=mesh, in_specs=in_specs, out_specs=out_specs, check_vma=False)
```

```python
import functools

import jax
import jax.numpy as jnp
from jax import lax
from jax.experimental import pallas as pl
from jax.experimental.pallas import tpu as pltpu
from jax.sharding import PartitionSpec as P

MESH = pl.DeviceIdType.MESH
STEPS = 4
NVAR = 4
PAD = 8
LANES = 128
WIDE = 256
CHUNK = 1024


def advance(source, target, kappa, keep, f, starts):
    tiles = source.shape[1]
    lane = lax.broadcasted_iota(jnp.int32, (8, LANES), 1)
    first, last = lane == 0, lane == LANES - 1
    for r in starts:
        here = [source[f, j, pl.ds(r, 8), :] for j in range(tiles)]
        right = [pltpu.roll(a, 1, 1) for a in here]
        left = [pltpu.roll(a, LANES - 1, 1) for a in here]
        for j in range(tiles):
            before = jnp.where(first, right[j - 1] if j else 0.0, right[j])
            after = jnp.where(last, left[j + 1] if j < tiles - 1 else 0.0, left[j])
            around = (source[f, j, pl.ds(r - 1, 8), :] + source[f, j, pl.ds(r + 1, 8), :]) + (before + after)
            target[f, j, pl.ds(r, 8), :] = keep[j, pl.ds(r, 8), :] * here[j] + kappa[j, pl.ds(r, 8), :] * around


def inner_rows(stages, kappa, keep, f, rows):
    for s in range(STEPS):
        advance(stages[s], stages[s + 1], kappa, keep, f, range(PAD, PAD + rows, 8))


def border_rows(stages, kappa, keep, fields, rows):
    for s in range(STEPS):
        for f in fields:
            advance(stages[s], stages[s + 1], kappa, keep, f, (PAD - STEPS + s, PAD + rows - STEPS - s))


def kernel(
    tiles,
    members,
    alpha_hbm,
    static_hbm,
    pert_hbm,
    table_hbm,
    class_hbm,
    cells_hbm,
    counts_hbm,
    innov_hbm,
    weights_hbm,
    out_alpha,
    out_static,
    alpha,
    static,
    pert,
    classes,
    cells,
    innov,
    weights,
    table,
    counts,
    kappa,
    keep,
    inverse,
    fwd0,
    fwd1,
    fwd2,
    fwd3,
    fwd4,
    adj0,
    adj1,
    adj2,
    adj3,
    adj4,
    fwd_send,
    fwd_recv,
    static_send,
    static_recv,
    wide_send,
    wide_recv,
    adj_send,
    adj_recv,
    field,
    split,
    hot_lane,
    hot_row,
    obs,
    pair_buf,
    ring_buf,
    resid,
    in_sem,
    fwd_sems,
    static_sems,
    wide_sems,
    adj_sems,
    pair_sems,
    ring_sems,
    swap_sems,
):
    owned, rows, cols = alpha.shape
    lane_tiles = cols // LANES
    folds = cols // WIDE
    field_rows = NVAR * rows
    depth = members // 4
    slots = cells.shape[0]
    half = slots // 2
    scale = (owned * members - 1.0) ** (-0.5)
    fwd = (fwd0, fwd1, fwd2, fwd3, fwd4)
    adj = (adj0, adj1, adj2, adj3, adj4)
    m = lax.axis_index("mem")
    t = lax.axis_index("tile")
    core = lax.rem(m, 2)
    quad = lax.rem(m, 4)
    far = quad // 2
    level = m // 4
    stride = members // NVAR
    owner = lax.rem(m, stride) == stride // 2
    var = m // stride
    has_up = t > 0
    has_down = t < tiles - 1

    core_mate = m + 1 - 2 * core
    far_mate = m + 2 - 4 * far
    both_mate = core_mate + 2 - 4 * far

    barrier = pltpu.get_barrier_semaphore()

    @pl.when(has_up)
    def _():
        pl.semaphore_signal(barrier, inc=1, device_id={"tile": t - 1}, device_id_type=MESH)

    @pl.when(has_down)
    def _():
        pl.semaphore_signal(barrier, inc=1, device_id={"tile": t + 1}, device_id_type=MESH)

    for mate in (core_mate, far_mate, both_mate):
        pl.semaphore_signal(barrier, inc=1, device_id={"mem": mate}, device_id_type=MESH)
    for d in range(1, depth):
        mate = lax.rem(level + d, depth) * 4 + quad
        pl.semaphore_signal(barrier, inc=1, device_id={"mem": mate}, device_id_type=MESH)

    loads = [
        pltpu.make_async_copy(class_hbm, classes, in_sem.at[0]),
        pltpu.make_async_copy(table_hbm, table, in_sem.at[1]),
        pltpu.make_async_copy(alpha_hbm, alpha, in_sem.at[2]),
        pltpu.make_async_copy(static_hbm, static, in_sem.at[3]),
        pltpu.make_async_copy(cells_hbm, cells, in_sem.at[4]),
        pltpu.make_async_copy(counts_hbm, counts, in_sem.at[5]),
        pltpu.make_async_copy(innov_hbm, innov, in_sem.at[6]),
        pltpu.make_async_copy(weights_hbm, weights, in_sem.at[7]),
        pltpu.make_async_copy(pert_hbm, pert, in_sem.at[8]),
    ]
    for load in loads:
        load.start()

    for edge, missing in ((0, t == 0), (1, t == tiles - 1)):

        @pl.when(missing)
        def _():
            fwd_recv[edge] = jnp.zeros(fwd_recv.shape[1:], jnp.float32)
            static_recv[edge] = jnp.zeros(static_recv.shape[1:], jnp.float32)
            wide_recv[edge] = jnp.zeros(wide_recv.shape[1:], jnp.float32)
            adj_recv[edge] = jnp.zeros(adj_recv.shape[1:], jnp.float32)

    def exchange(send, recv, sems):
        up = pltpu.make_async_remote_copy(
            send.at[0], recv.at[1], sems.at[0, 0], sems.at[1, 1], device_id={"tile": t - 1}, device_id_type=MESH
        )
        down = pltpu.make_async_remote_copy(
            send.at[1], recv.at[0], sems.at[0, 1], sems.at[1, 0], device_id={"tile": t + 1}, device_id_type=MESH
        )
        return up, down

    def start(pair):
        @pl.when(has_up)
        def _():
            pair[0].start()

        @pl.when(has_down)
        def _():
            pair[1].start()

    def wait(pair):
        @pl.when(has_up)
        def _():
            pair[0].wait_send()
            pair[1].wait_recv()

        @pl.when(has_down)
        def _():
            pair[1].wait_send()
            pair[0].wait_recv()

    def pack(send, g, top, bottom):
        at = pl.ds(4 * (g % 2), STEPS)
        send[0, g // 2, at, :] = top
        send[1, g // 2, at, :] = bottom

    def unpack(recv, g, target, index):
        at = pl.ds(4 * (g % 2), STEPS)
        target[(*index, pl.ds(PAD - STEPS, STEPS), slice(None))] = recv[0, g // 2, at, :]
        target[(*index, pl.ds(PAD + rows, STEPS), slice(None))] = recv[1, g // 2, at, :]

    own = pl.ds(PAD, rows)
    top_rows = pl.ds(PAD, STEPS)
    bottom_rows = pl.ds(PAD + rows - STEPS, STEPS)
    columns = [pl.ds(j * LANES, LANES) for j in range(lane_tiles)]

    loads[0].wait()
    loads[1].wait()
    for j in range(lane_tiles):
        kind = classes[:, columns[j]]
        value = jnp.full(kind.shape, table[0], jnp.float32)
        for i in range(1, table.shape[0]):
            value = jnp.where(kind == i, table[i], value)
        kappa[j, own, :] = value
        keep[j, own, :] = 1.0 - 4.0 * value
        pack(fwd_send, owned * lane_tiles + j, value[:STEPS], value[rows - STEPS :])
    loads[2].wait()
    for f in range(owned):
        for j in range(lane_tiles):
            fwd0[f, j, own, :] = alpha[f, :, columns[j]]
            pack(fwd_send, f * lane_tiles + j, fwd0[f, j, top_rows, :], fwd0[f, j, bottom_rows, :])
    loads[3].wait()

    @pl.when(owner)
    def _():
        for j in range(lane_tiles):
            fwd0[owned, j, own, :] = static[var, :, columns[j]]
            pack(static_send, j, fwd0[owned, j, top_rows, :], fwd0[owned, j, bottom_rows, :])

    pl.semaphore_wait(barrier, depth + 2 + has_up.astype(jnp.int32) + has_down.astype(jnp.int32))
    fwd_pair = exchange(fwd_send, fwd_recv, fwd_sems)
    start(fwd_pair)
    static_pair = exchange(static_send, static_recv, static_sems)

    @pl.when(owner)
    def _():
        start(static_pair)

    loads[4].wait()
    lane_of = lax.broadcasted_iota(jnp.int32, (WIDE, LANES), 0)
    three_rows = folds * lax.broadcasted_iota(jnp.int32, (field_rows, LANES), 0)

    def make_hot_lane(i, carry):
        at = pl.ds(pl.multiple_of(i * LANES, LANES), LANES)
        hot_lane[:, at] = jnp.where(lane_of == (cells[pl.ds(i, 1), :] & (WIDE - 1)), 1.0, 0.0).astype(jnp.bfloat16)
        return carry

    def make_hot_row(i, carry):
        at = pl.ds(pl.multiple_of(i * LANES, LANES), LANES)
        row = cells[pl.ds(i, 1), :] // WIDE
        for fold in range(folds):
            hot = jnp.where(three_rows == row - fold, 1.0, 0.0).astype(jnp.bfloat16)
            hot_row[pl.ds(fold * field_rows, field_rows), at] = hot
        return carry

    lax.fori_loop(0, slots, make_hot_lane, 0)

    def inner_fwd(f, carry):
        inner_rows(fwd, kappa, keep, f, rows)
        return carry

    lax.fori_loop(0, owned, inner_fwd, 0)

    @pl.when(owner)
    def _():
        inner_rows(fwd, kappa, keep, owned, rows)

    for load in loads[5:]:
        load.wait()

    wait(fwd_pair)
    for j in range(lane_tiles):
        unpack(fwd_recv, owned * lane_tiles + j, kappa, (j,))
        for at in (pl.ds(PAD - STEPS, STEPS), pl.ds(PAD + rows, STEPS)):
            keep[j, at, :] = 1.0 - 4.0 * kappa[j, at, :]
        for f in range(owned):
            unpack(fwd_recv, f * lane_tiles + j, fwd0, (f, j))
    border_rows(fwd, kappa, keep, range(owned), rows)

    def place(v, j):
        return pl.ds((j * LANES // WIDE) * field_rows + v * rows, rows), pl.ds(j * LANES % WIDE, LANES)

    for j in range(lane_tiles):
        for v in range(NVAR):
            total = pert[0, v, :, columns[j]].astype(jnp.float32) * fwd4[0, j, own, :]
            for f in range(1, owned):
                total = total + pert[f, v, :, columns[j]].astype(jnp.float32) * fwd4[f, j, own, :]
            field[place(v, j)] = scale * total

    @pl.when(owner)
    def _():
        wait(static_pair)
        for j in range(lane_tiles):
            unpack(static_recv, j, fwd0, (owned, j))
        border_rows(fwd, kappa, keep, (owned,), rows)
        for j in range(lane_tiles):
            at = place(0, j)
            at = (pl.ds(pl.multiple_of(at[0].start + var * rows, rows), rows), at[1])
            field[at] = field[at] + fwd4[owned, j, own, :]

    high = field[...].astype(jnp.bfloat16)
    split[0] = high
    split[1] = (field[...] - high.astype(jnp.float32)).astype(jnp.bfloat16)

    per_chunk = CHUNK // LANES
    row_chunk = folds * lax.broadcasted_iota(jnp.int32, (field_rows, CHUNK), 0)

    def pick(i, carry):
        at = pl.ds(pl.multiple_of(i * CHUNK, CHUNK), CHUNK)
        hot = hot_lane[:, at]
        found = jnp.dot(split[0], hot, preferred_element_type=jnp.float32)
        found = found + jnp.dot(split[1], hot, preferred_element_type=jnp.float32)
        row = jnp.concatenate([cells[pl.ds(per_chunk * i + q, 1), :] for q in range(per_chunk)], 1) // WIDE
        kept = jnp.zeros((field_rows, CHUNK), jnp.float32)
        for fold in range(folds):
            kept = jnp.where(row_chunk == row - fold, found[fold * field_rows : (fold + 1) * field_rows], kept)
        value = jnp.sum(kept, 0, keepdims=True)
        for q in range(per_chunk):
            obs[pl.ds(per_chunk * i + q, 1), :] = value[:, q * LANES : (q + 1) * LANES]
        return carry

    mine = pl.ds(pl.multiple_of(core * half, 8), half)
    others = pl.ds(pl.multiple_of((1 - core) * half, 8), half)
    blocks = half // per_chunk

    def pair_copy(source, mate, sender, at):
        return pltpu.make_async_remote_copy(
            source, pair_buf.at[sender], pair_sems.at[0, at], pair_sems.at[1, sender], device_id={"mem": mate}, device_id_type=MESH
        )

    lax.fori_loop((1 - core) * blocks, (2 - core) * blocks, pick, 0)
    pair_both = pair_copy(obs.at[others], both_mate, quad, 1)
    pair_core = pair_copy(obs.at[others], core_mate, quad, 0)
    pair_both.start()
    pair_core.start()
    lax.fori_loop(core * blocks, (core + 1) * blocks, pick, 0)
    pair_far = pair_copy(obs.at[mine], far_mate, quad, 2)
    pair_far.start()
    pair_buf[quad] = obs[mine]
    for mate in (core_mate, far_mate, both_mate):
        pair_copy(obs.at[mine], mate, lax.rem(mate, 4), 0).wait_recv()
    ring_buf[level] = pair_buf[0] + pair_buf[1] + pair_buf[2] + pair_buf[3]

    def ring_copy(d):
        to = lax.rem(level + d, depth) * 4 + quad
        return pltpu.make_async_remote_copy(
            ring_buf.at[level], ring_buf.at[level], ring_sems.at[0, d], ring_sems.at[1, level], device_id={"mem": to}, device_id_type=MESH
        )

    order = sorted(range(1, depth), key=lambda d: -min(d, depth - d))
    for d in order:
        ring_copy(d).start()
    lax.fori_loop(0, slots, make_hot_row, 0)
    for j in range(lane_tiles):
        inverse[j] = 1.0 / kappa[j, own, :]
    for d in range(1, depth):
        other = lax.rem(level + d, depth)
        pltpu.make_async_remote_copy(
            ring_buf.at[other],
            ring_buf.at[other],
            ring_sems.at[0, d],
            ring_sems.at[1, other],
            device_id={"mem": other * 4 + quad},
            device_id_type=MESH,
        ).wait_recv()
    observed = ring_buf[0]
    for d in range(1, depth):
        observed = observed + ring_buf[d]
    slot = lax.broadcasted_iota(jnp.int32, (half, LANES), 0) * LANES + lax.broadcasted_iota(jnp.int32, (half, LANES), 1)
    slot = slot + core * (half * LANES)
    resid[mine] = jnp.where(slot < counts[0], (observed - innov[mine]) * weights[mine], 0.0)
    swap = pltpu.make_async_remote_copy(
        resid.at[mine], resid.at[mine], swap_sems.at[0], swap_sems.at[1], device_id={"mem": core_mate}, device_id_type=MESH
    )
    swap.start()

    def spread(which):
        at = pl.ds(pl.multiple_of(which * (half * LANES), half * LANES), half * LANES)
        value = jnp.concatenate([resid[pl.ds(which * half + q, 1), :] for q in range(half)], 1)
        high = value.astype(jnp.bfloat16)
        low = (value - high.astype(jnp.float32)).astype(jnp.bfloat16)
        hot = hot_lane[:, at]
        row = hot_row[:, at]
        return lax.dot_general(
            jnp.concatenate([row, row], 1),
            jnp.concatenate([hot * high, hot * low], 1),
            (((1,), (1,)), ((), ())),
            preferred_element_type=jnp.float32,
        )

    field[...] = spread(core)
    swap.wait()
    field[...] = field[...] + spread(1 - core)

    for j in range(lane_tiles):
        for v in range(NVAR):
            adj0[owned + v, j, own, :] = kappa[j, own, :] * field[place(v, j)]
            pack(wide_send, v * lane_tiles + j, adj0[owned + v, j, top_rows, :], adj0[owned + v, j, bottom_rows, :])
    wide_pair = exchange(wide_send, wide_recv, wide_sems)
    start(wide_pair)
    for j in range(lane_tiles):
        for f in range(owned):
            total = pert[f, 0, :, columns[j]].astype(jnp.float32) * field[place(0, j)]
            for v in range(1, NVAR):
                total = total + pert[f, v, :, columns[j]].astype(jnp.float32) * field[place(v, j)]
            adj0[f, j, own, :] = kappa[j, own, :] * (scale * total)
            pack(adj_send, f * lane_tiles + j, adj0[f, j, top_rows, :], adj0[f, j, bottom_rows, :])
    adj_pair = exchange(adj_send, adj_recv, adj_sems)
    start(adj_pair)

    def inner_adj(f, carry):
        inner_rows(adj, kappa, keep, f, rows)
        return carry

    lax.fori_loop(0, owned + NVAR, inner_adj, 0)
    pair_core.wait_send()
    pair_both.wait_send()
    pair_far.wait_send()
    for d in range(1, depth):
        ring_copy(d).wait_send()
    wait(wide_pair)
    for j in range(lane_tiles):
        for v in range(NVAR):
            unpack(wide_recv, v * lane_tiles + j, adj0, (owned + v, j))
    border_rows(adj, kappa, keep, range(owned, owned + NVAR), rows)
    for j in range(lane_tiles):
        for v in range(NVAR):
            out_static[v, :, columns[j]] = static[v, :, columns[j]] + adj4[owned + v, j, own, :] * inverse[j]
    wait(adj_pair)
    for j in range(lane_tiles):
        for f in range(owned):
            unpack(adj_recv, f * lane_tiles + j, adj0, (f, j))
    border_rows(adj, kappa, keep, range(owned), rows)
    for j in range(lane_tiles):
        for f in range(owned):
            out_alpha[f, :, columns[j]] = alpha[f, :, columns[j]] + adj4[f, j, own, :] * inverse[j]


def write_out(alpha, static, out_alpha, out_static, sems):
    copies = [pltpu.make_async_copy(alpha, out_alpha, sems.at[0]), pltpu.make_async_copy(static, out_static, sems.at[1])]
    for copy in copies:
        copy.start()
    for copy in copies:
        copy.wait()


def body(tiles, members, alpha_fields, static_control, perturbations, coef_table, coef_class, obs_cells, obs_counts, innovations, obs_weights):
    owned, rows, cols = alpha_fields.shape
    slots = obs_cells.shape[1] // LANES
    folded = (slots, LANES)
    half = slots // 2
    depth = members // 4
    fields = owned + NVAR
    lane_tiles = cols // LANES
    deep = rows + 2 * PAD
    field_rows = cols // WIDE * NVAR * rows
    f32, bf16, i32 = jnp.float32, jnp.bfloat16, jnp.int32
    anywhere = pl.BlockSpec(memory_space=pl.ANY)
    in_hbm = functools.partial(pltpu.with_memory_space_constraint, memory_space=pltpu.HBM)
    in_vmem = pl.BlockSpec(memory_space=pltpu.VMEM)
    dma = pltpu.SemaphoreType.DMA

    def message(count):
        return [pltpu.VMEM((2, count * lane_tiles // 2, 8, LANES), f32)] * 2

    shapes = (jax.ShapeDtypeStruct((owned, rows, cols), f32), jax.ShapeDtypeStruct((NVAR, rows, cols), f32))
    grads = pl.pallas_call(
        functools.partial(kernel, tiles, members),
        out_shape=shapes,
        in_specs=[anywhere] * 9,
        out_specs=(in_vmem, in_vmem),
        scratch_shapes=[
            pltpu.VMEM((owned, rows, cols), f32),
            pltpu.VMEM((NVAR, rows, cols), f32),
            pltpu.VMEM((owned, NVAR, rows, cols), bf16),
            pltpu.VMEM((rows, cols), i32),
            pltpu.VMEM(folded, i32),
            pltpu.VMEM(folded, f32),
            pltpu.VMEM(folded, f32),
            pltpu.SMEM(coef_table.shape, f32),
            pltpu.SMEM(obs_counts.shape, i32),
            pltpu.VMEM((lane_tiles, deep, LANES), f32),
            pltpu.VMEM((lane_tiles, deep, LANES), f32),
            pltpu.VMEM((lane_tiles, rows, LANES), f32),
            *[pltpu.VMEM((owned + 1, lane_tiles, deep, LANES), f32)] * (STEPS + 1),
            *[pltpu.VMEM((fields, lane_tiles, deep, LANES), f32)] * (STEPS + 1),
            *message(owned + 1),
            *message(1),
            *message(NVAR),
            *message(owned),
            pltpu.VMEM((field_rows, WIDE), f32),
            pltpu.VMEM((2, field_rows, WIDE), bf16),
            pltpu.VMEM((WIDE, slots * LANES), bf16),
            pltpu.VMEM((field_rows, slots * LANES), bf16),
            pltpu.VMEM(folded, f32),
            pltpu.VMEM((4, half, LANES), f32),
            pltpu.VMEM((depth, half, LANES), f32),
            pltpu.VMEM(folded, f32),
            dma((9,)),
            dma((2, 2)),
            dma((2, 2)),
            dma((2, 2)),
            dma((2, 2)),
            dma((2, 4)),
            dma((2, depth)),
            dma((2,)),
        ],
        compiler_params=pltpu.CompilerParams(collective_id=0, has_side_effects=True, vmem_limit_bytes=48 * 2**20),
    )(
        in_hbm(alpha_fields),
        in_hbm(static_control),
        in_hbm(perturbations),
        in_hbm(coef_table),
        in_hbm(coef_class),
        in_hbm(obs_cells.reshape(folded)),
        obs_counts,
        in_hbm(innovations.reshape(folded)),
        in_hbm(obs_weights.reshape(folded)),
    )
    return pl.pallas_call(
        write_out,
        out_shape=shapes,
        in_specs=[anywhere, anywhere],
        out_specs=(anywhere, anywhere),
        scratch_shapes=[dma((2,))],
        compiler_params=pltpu.CompilerParams(vmem_limit_bytes=2**20),
    )(*grads)


def solution(mesh):
    in_specs = (
        P("mem", "tile", None),
        P(None, "tile", None),
        P("mem", None, "tile", None),
        P(),
        P("tile", None),
        P("tile", None),
        P("tile"),
        P("tile", None),
        P("tile", None),
    )
    out_specs = (P("mem", "tile", None), P(None, "tile", None))
    run = functools.partial(body, mesh.shape["tile"], mesh.shape["mem"])
    return jax.shard_map(run, mesh=mesh, in_specs=in_specs, out_specs=out_specs, check_vma=False)
```

```python
import functools

import jax
import jax.numpy as jnp
from jax import lax
from jax.experimental import pallas as pl
from jax.experimental.pallas import tpu as pltpu
from jax.sharding import PartitionSpec as P

MESH = pl.DeviceIdType.MESH
STEPS = 4
NVAR = 4
PAD = 8
LANES = 128
WIDE = 256
CHUNK = 1024


def advance(source, target, kappa, keep, f, starts):
    tiles = source.shape[1]
    lane = lax.broadcasted_iota(jnp.int32, (8, LANES), 1)
    first, last = lane == 0, lane == LANES - 1
    for r in starts:
        here = [source[f, j, pl.ds(r, 8), :] for j in range(tiles)]
        right = [pltpu.roll(a, 1, 1) for a in here]
        left = [pltpu.roll(a, LANES - 1, 1) for a in here]
        for j in range(tiles):
            before = jnp.where(first, right[j - 1] if j else 0.0, right[j])
            after = jnp.where(last, left[j + 1] if j < tiles - 1 else 0.0, left[j])
            around = (source[f, j, pl.ds(r - 1, 8), :] + source[f, j, pl.ds(r + 1, 8), :]) + (before + after)
            target[f, j, pl.ds(r, 8), :] = keep[j, pl.ds(r, 8), :] * here[j] + kappa[j, pl.ds(r, 8), :] * around


def inner_rows(stages, kappa, keep, f, rows):
    for s in range(STEPS):
        advance(stages[s], stages[s + 1], kappa, keep, f, range(PAD, PAD + rows, 8))


def border_rows(stages, kappa, keep, fields, rows):
    tiles = kappa.shape[0]
    lane = lax.broadcasted_iota(jnp.int32, (8, LANES), 1)
    first, last = lane == 0, lane == LANES - 1
    upper = lax.broadcasted_iota(jnp.int32, (8, LANES), 0) < 4
    for s in range(STEPS):
        top, bottom = PAD - 3 + s, PAD + rows - 1 - s

        def both(ref, index, shift):
            return jnp.where(upper, ref[(*index, pl.ds(top + shift, 8))], ref[(*index, pl.ds(bottom - 4 + shift, 8))])

        factor = [both(kappa, (j,), 0) for j in range(tiles)]
        kept = [both(keep, (j,), 0) for j in range(tiles)]
        source, target = stages[s], stages[s + 1]
        for f in fields:
            here = [both(source, (f, j), 0) for j in range(tiles)]
            right = [pltpu.roll(a, 1, 1) for a in here]
            left = [pltpu.roll(a, LANES - 1, 1) for a in here]
            for j in range(tiles):
                before = jnp.where(first, right[j - 1] if j else 0.0, right[j])
                after = jnp.where(last, left[j + 1] if j < tiles - 1 else 0.0, left[j])
                around = (both(source, (f, j), -1) + both(source, (f, j), 1)) + (before + after)
                value = kept[j] * here[j] + factor[j] * around
                target[f, j, pl.ds(top, 4), :] = value[:4]
                target[f, j, pl.ds(bottom, 4), :] = value[4:]


def kernel(
    tiles,
    members,
    alpha_hbm,
    static_hbm,
    pert_hbm,
    table_hbm,
    class_hbm,
    cells_hbm,
    counts_hbm,
    innov_hbm,
    weights_hbm,
    out_alpha,
    out_static,
    alpha,
    static,
    pert,
    classes,
    cells,
    innov,
    weights,
    table,
    counts,
    kappa,
    keep,
    inverse,
    fwd0,
    fwd1,
    fwd2,
    fwd3,
    fwd4,
    adj0,
    adj1,
    adj2,
    adj3,
    adj4,
    fwd_send,
    fwd_recv,
    static_send,
    static_recv,
    wide_send,
    wide_recv,
    adj_send,
    adj_recv,
    field,
    split,
    hot_lane,
    hot_row,
    obs,
    pair_buf,
    ring_buf,
    resid,
    in_sem,
    fwd_sems,
    static_sems,
    wide_sems,
    adj_sems,
    pair_sems,
    ring_sems,
    swap_sems,
):
    owned, rows, cols = alpha.shape
    lane_tiles = cols // LANES
    folds = cols // WIDE
    field_rows = NVAR * rows
    depth = members // 4
    slots = cells.shape[0]
    half = slots // 2
    scale = (owned * members - 1.0) ** (-0.5)
    fwd = (fwd0, fwd1, fwd2, fwd3, fwd4)
    adj = (adj0, adj1, adj2, adj3, adj4)
    m = lax.axis_index("mem")
    t = lax.axis_index("tile")
    core = lax.rem(m, 2)
    quad = lax.rem(m, 4)
    far = quad // 2
    level = m // 4
    stride = members // NVAR
    owner = lax.rem(m, stride) == stride // 2
    var = m // stride
    has_up = t > 0
    has_down = t < tiles - 1

    core_mate = m + 1 - 2 * core
    far_mate = m + 2 - 4 * far
    both_mate = core_mate + 2 - 4 * far

    barrier = pltpu.get_barrier_semaphore()

    @pl.when(has_up)
    def _():
        pl.semaphore_signal(barrier, inc=1, device_id={"tile": t - 1}, device_id_type=MESH)

    @pl.when(has_down)
    def _():
        pl.semaphore_signal(barrier, inc=1, device_id={"tile": t + 1}, device_id_type=MESH)

    for mate in (core_mate, far_mate, both_mate):
        pl.semaphore_signal(barrier, inc=1, device_id={"mem": mate}, device_id_type=MESH)
    for d in range(1, depth):
        mate = lax.rem(level + d, depth) * 4 + quad
        pl.semaphore_signal(barrier, inc=1, device_id={"mem": mate}, device_id_type=MESH)

    loads = [
        pltpu.make_async_copy(class_hbm, classes, in_sem.at[0]),
        pltpu.make_async_copy(table_hbm, table, in_sem.at[1]),
        pltpu.make_async_copy(alpha_hbm, alpha, in_sem.at[2]),
        pltpu.make_async_copy(static_hbm, static, in_sem.at[3]),
        pltpu.make_async_copy(cells_hbm, cells, in_sem.at[4]),
        pltpu.make_async_copy(counts_hbm, counts, in_sem.at[5]),
        pltpu.make_async_copy(innov_hbm, innov, in_sem.at[6]),
        pltpu.make_async_copy(weights_hbm, weights, in_sem.at[7]),
        pltpu.make_async_copy(pert_hbm, pert, in_sem.at[8]),
    ]
    for load in loads:
        load.start()

    for edge, missing in ((0, t == 0), (1, t == tiles - 1)):

        @pl.when(missing)
        def _():
            fwd_recv[edge] = jnp.zeros(fwd_recv.shape[1:], jnp.float32)
            static_recv[edge] = jnp.zeros(static_recv.shape[1:], jnp.float32)
            wide_recv[edge] = jnp.zeros(wide_recv.shape[1:], jnp.float32)
            adj_recv[edge] = jnp.zeros(adj_recv.shape[1:], jnp.float32)

    def exchange(send, recv, sems):
        up = pltpu.make_async_remote_copy(
            send.at[0], recv.at[1], sems.at[0, 0], sems.at[1, 1], device_id={"tile": t - 1}, device_id_type=MESH
        )
        down = pltpu.make_async_remote_copy(
            send.at[1], recv.at[0], sems.at[0, 1], sems.at[1, 0], device_id={"tile": t + 1}, device_id_type=MESH
        )
        return up, down

    def start(pair):
        @pl.when(has_up)
        def _():
            pair[0].start()

        @pl.when(has_down)
        def _():
            pair[1].start()

    def wait(pair):
        @pl.when(has_up)
        def _():
            pair[0].wait_send()
            pair[1].wait_recv()

        @pl.when(has_down)
        def _():
            pair[1].wait_send()
            pair[0].wait_recv()

    def pack(send, g, top, bottom):
        at = pl.ds(4 * (g % 2), STEPS)
        send[0, g // 2, at, :] = top
        send[1, g // 2, at, :] = bottom

    def unpack(recv, g, target, index):
        at = pl.ds(4 * (g % 2), STEPS)
        target[(*index, pl.ds(PAD - STEPS, STEPS), slice(None))] = recv[0, g // 2, at, :]
        target[(*index, pl.ds(PAD + rows, STEPS), slice(None))] = recv[1, g // 2, at, :]

    own = pl.ds(PAD, rows)
    top_rows = pl.ds(PAD, STEPS)
    bottom_rows = pl.ds(PAD + rows - STEPS, STEPS)
    columns = [pl.ds(j * LANES, LANES) for j in range(lane_tiles)]

    loads[0].wait()
    loads[1].wait()
    for j in range(lane_tiles):
        kind = classes[:, columns[j]]
        value = jnp.full(kind.shape, table[0], jnp.float32)
        for i in range(1, table.shape[0]):
            value = jnp.where(kind == i, table[i], value)
        kappa[j, own, :] = value
        keep[j, own, :] = 1.0 - 4.0 * value
        pack(fwd_send, owned * lane_tiles + j, value[:STEPS], value[rows - STEPS :])
    loads[2].wait()
    for f in range(owned):
        for j in range(lane_tiles):
            fwd0[f, j, own, :] = alpha[f, :, columns[j]]
            pack(fwd_send, f * lane_tiles + j, fwd0[f, j, top_rows, :], fwd0[f, j, bottom_rows, :])
    loads[3].wait()

    @pl.when(owner)
    def _():
        for j in range(lane_tiles):
            fwd0[owned, j, own, :] = static[var, :, columns[j]]
            pack(static_send, j, fwd0[owned, j, top_rows, :], fwd0[owned, j, bottom_rows, :])

    pl.semaphore_wait(barrier, depth + 2 + has_up.astype(jnp.int32) + has_down.astype(jnp.int32))
    fwd_pair = exchange(fwd_send, fwd_recv, fwd_sems)
    start(fwd_pair)
    static_pair = exchange(static_send, static_recv, static_sems)

    @pl.when(owner)
    def _():
        start(static_pair)

    loads[4].wait()
    lane_of = lax.broadcasted_iota(jnp.int32, (WIDE, LANES), 0)
    three_rows = folds * lax.broadcasted_iota(jnp.int32, (field_rows, LANES), 0)

    def make_hot_lane(i, carry):
        at = pl.ds(pl.multiple_of(i * LANES, LANES), LANES)
        hot_lane[:, at] = jnp.where(lane_of == (cells[pl.ds(i, 1), :] & (WIDE - 1)), 1.0, 0.0).astype(jnp.bfloat16)
        return carry

    def make_hot_row(i, carry):
        at = pl.ds(pl.multiple_of(i * LANES, LANES), LANES)
        row = cells[pl.ds(i, 1), :] // WIDE
        for fold in range(folds):
            hot = jnp.where(three_rows == row - fold, 1.0, 0.0).astype(jnp.bfloat16)
            hot_row[pl.ds(fold * field_rows, field_rows), at] = hot
        return carry

    lax.fori_loop(0, slots, make_hot_lane, 0)

    def inner_fwd(f, carry):
        inner_rows(fwd, kappa, keep, f, rows)
        return carry

    lax.fori_loop(0, owned, inner_fwd, 0)

    @pl.when(owner)
    def _():
        inner_rows(fwd, kappa, keep, owned, rows)

    for load in loads[5:]:
        load.wait()

    wait(fwd_pair)
    for j in range(lane_tiles):
        unpack(fwd_recv, owned * lane_tiles + j, kappa, (j,))
        for at in (pl.ds(PAD - STEPS, STEPS), pl.ds(PAD + rows, STEPS)):
            keep[j, at, :] = 1.0 - 4.0 * kappa[j, at, :]
        for f in range(owned):
            unpack(fwd_recv, f * lane_tiles + j, fwd0, (f, j))
    border_rows(fwd, kappa, keep, range(owned), rows)

    def place(v, j):
        return pl.ds((j * LANES // WIDE) * field_rows + v * rows, rows), pl.ds(j * LANES % WIDE, LANES)

    for j in range(lane_tiles):
        for v in range(NVAR):
            total = pert[0, v, :, columns[j]].astype(jnp.float32) * fwd4[0, j, own, :]
            for f in range(1, owned):
                total = total + pert[f, v, :, columns[j]].astype(jnp.float32) * fwd4[f, j, own, :]
            field[place(v, j)] = scale * total

    @pl.when(owner)
    def _():
        wait(static_pair)
        for j in range(lane_tiles):
            unpack(static_recv, j, fwd0, (owned, j))
        border_rows(fwd, kappa, keep, (owned,), rows)
        for j in range(lane_tiles):
            at = place(0, j)
            at = (pl.ds(pl.multiple_of(at[0].start + var * rows, rows), rows), at[1])
            field[at] = field[at] + fwd4[owned, j, own, :]

    high = field[...].astype(jnp.bfloat16)
    split[0] = high
    split[1] = (field[...] - high.astype(jnp.float32)).astype(jnp.bfloat16)

    per_chunk = CHUNK // LANES
    row_chunk = folds * lax.broadcasted_iota(jnp.int32, (field_rows, CHUNK), 0)

    def pick(i, carry):
        at = pl.ds(pl.multiple_of(i * CHUNK, CHUNK), CHUNK)
        hot = hot_lane[:, at]
        found = jnp.dot(split[0], hot, preferred_element_type=jnp.float32)
        found = found + jnp.dot(split[1], hot, preferred_element_type=jnp.float32)
        row = jnp.concatenate([cells[pl.ds(per_chunk * i + q, 1), :] for q in range(per_chunk)], 1) // WIDE
        kept = jnp.zeros((field_rows, CHUNK), jnp.float32)
        for fold in range(folds):
            kept = jnp.where(row_chunk == row - fold, found[fold * field_rows : (fold + 1) * field_rows], kept)
        value = jnp.sum(kept, 0, keepdims=True)
        for q in range(per_chunk):
            obs[pl.ds(per_chunk * i + q, 1), :] = value[:, q * LANES : (q + 1) * LANES]
        return carry

    mine = pl.ds(pl.multiple_of(core * half, 8), half)
    others = pl.ds(pl.multiple_of((1 - core) * half, 8), half)
    blocks = half // per_chunk

    def pair_copy(source, mate, sender, at):
        return pltpu.make_async_remote_copy(
            source, pair_buf.at[sender], pair_sems.at[0, at], pair_sems.at[1, sender], device_id={"mem": mate}, device_id_type=MESH
        )

    lax.fori_loop((1 - core) * blocks, (2 - core) * blocks, pick, 0)
    pair_both = pair_copy(obs.at[others], both_mate, quad, 1)
    pair_core = pair_copy(obs.at[others], core_mate, quad, 0)
    pair_both.start()
    pair_core.start()
    lax.fori_loop(core * blocks, (core + 1) * blocks, pick, 0)
    pair_far = pair_copy(obs.at[mine], far_mate, quad, 2)
    pair_far.start()
    pair_buf[quad] = obs[mine]
    for mate in (core_mate, far_mate, both_mate):
        pair_copy(obs.at[mine], mate, lax.rem(mate, 4), 0).wait_recv()
    ring_buf[level] = pair_buf[0] + pair_buf[1] + pair_buf[2] + pair_buf[3]

    def ring_copy(d):
        to = lax.rem(level + d, depth) * 4 + quad
        return pltpu.make_async_remote_copy(
            ring_buf.at[level], ring_buf.at[level], ring_sems.at[0, d], ring_sems.at[1, level], device_id={"mem": to}, device_id_type=MESH
        )

    order = sorted(range(1, depth), key=lambda d: -min(d, depth - d))
    for d in order:
        ring_copy(d).start()
    lax.fori_loop(0, slots, make_hot_row, 0)
    for j in range(lane_tiles):
        inverse[j] = 1.0 / kappa[j, own, :]
    for d in range(1, depth):
        other = lax.rem(level + d, depth)
        pltpu.make_async_remote_copy(
            ring_buf.at[other],
            ring_buf.at[other],
            ring_sems.at[0, d],
            ring_sems.at[1, other],
            device_id={"mem": other * 4 + quad},
            device_id_type=MESH,
        ).wait_recv()
    observed = ring_buf[0]
    for d in range(1, depth):
        observed = observed + ring_buf[d]
    slot = lax.broadcasted_iota(jnp.int32, (half, LANES), 0) * LANES + lax.broadcasted_iota(jnp.int32, (half, LANES), 1)
    slot = slot + core * (half * LANES)
    resid[mine] = jnp.where(slot < counts[0], (observed - innov[mine]) * weights[mine], 0.0)
    swap = pltpu.make_async_remote_copy(
        resid.at[mine], resid.at[mine], swap_sems.at[0], swap_sems.at[1], device_id={"mem": core_mate}, device_id_type=MESH
    )
    swap.start()

    def spread(which):
        at = pl.ds(pl.multiple_of(which * (half * LANES), half * LANES), half * LANES)
        value = jnp.concatenate([resid[pl.ds(which * half + q, 1), :] for q in range(half)], 1)
        high = value.astype(jnp.bfloat16)
        low = (value - high.astype(jnp.float32)).astype(jnp.bfloat16)
        hot = hot_lane[:, at]
        row = hot_row[:, at]
        return lax.dot_general(
            jnp.concatenate([row, row], 1),
            jnp.concatenate([hot * high, hot * low], 1),
            (((1,), (1,)), ((), ())),
            preferred_element_type=jnp.float32,
        )

    field[...] = spread(core)
    swap.wait()
    field[...] = field[...] + spread(1 - core)

    for j in range(lane_tiles):
        for v in range(NVAR):
            adj0[owned + v, j, own, :] = kappa[j, own, :] * field[place(v, j)]
            pack(wide_send, v * lane_tiles + j, adj0[owned + v, j, top_rows, :], adj0[owned + v, j, bottom_rows, :])
    wide_pair = exchange(wide_send, wide_recv, wide_sems)
    start(wide_pair)
    for j in range(lane_tiles):
        for f in range(owned):
            total = pert[f, 0, :, columns[j]].astype(jnp.float32) * field[place(0, j)]
            for v in range(1, NVAR):
                total = total + pert[f, v, :, columns[j]].astype(jnp.float32) * field[place(v, j)]
            adj0[f, j, own, :] = kappa[j, own, :] * (scale * total)
            pack(adj_send, f * lane_tiles + j, adj0[f, j, top_rows, :], adj0[f, j, bottom_rows, :])
    adj_pair = exchange(adj_send, adj_recv, adj_sems)
    start(adj_pair)

    def inner_adj(f, carry):
        inner_rows(adj, kappa, keep, f, rows)
        return carry

    lax.fori_loop(0, owned + NVAR, inner_adj, 0)
    pair_core.wait_send()
    pair_both.wait_send()
    pair_far.wait_send()
    for d in range(1, depth):
        ring_copy(d).wait_send()
    wait(wide_pair)
    for j in range(lane_tiles):
        for v in range(NVAR):
            unpack(wide_recv, v * lane_tiles + j, adj0, (owned + v, j))
    border_rows(adj, kappa, keep, range(owned, owned + NVAR), rows)
    for j in range(lane_tiles):
        for v in range(NVAR):
            out_static[v, :, columns[j]] = static[v, :, columns[j]] + adj4[owned + v, j, own, :] * inverse[j]
    wait(adj_pair)
    for j in range(lane_tiles):
        for f in range(owned):
            unpack(adj_recv, f * lane_tiles + j, adj0, (f, j))
    border_rows(adj, kappa, keep, range(owned), rows)
    for j in range(lane_tiles):
        for f in range(owned):
            out_alpha[f, :, columns[j]] = alpha[f, :, columns[j]] + adj4[f, j, own, :] * inverse[j]


def write_out(alpha, static, out_alpha, out_static, sems):
    copies = [pltpu.make_async_copy(alpha, out_alpha, sems.at[0]), pltpu.make_async_copy(static, out_static, sems.at[1])]
    for copy in copies:
        copy.start()
    for copy in copies:
        copy.wait()


def body(tiles, members, alpha_fields, static_control, perturbations, coef_table, coef_class, obs_cells, obs_counts, innovations, obs_weights):
    owned, rows, cols = alpha_fields.shape
    slots = obs_cells.shape[1] // LANES
    folded = (slots, LANES)
    half = slots // 2
    depth = members // 4
    fields = owned + NVAR
    lane_tiles = cols // LANES
    deep = rows + 2 * PAD
    field_rows = cols // WIDE * NVAR * rows
    f32, bf16, i32 = jnp.float32, jnp.bfloat16, jnp.int32
    anywhere = pl.BlockSpec(memory_space=pl.ANY)
    in_hbm = functools.partial(pltpu.with_memory_space_constraint, memory_space=pltpu.HBM)
    in_vmem = pl.BlockSpec(memory_space=pltpu.VMEM)
    dma = pltpu.SemaphoreType.DMA

    def message(count):
        return [pltpu.VMEM((2, count * lane_tiles // 2, 8, LANES), f32)] * 2

    shapes = (jax.ShapeDtypeStruct((owned, rows, cols), f32), jax.ShapeDtypeStruct((NVAR, rows, cols), f32))
    grads = pl.pallas_call(
        functools.partial(kernel, tiles, members),
        out_shape=shapes,
        in_specs=[anywhere] * 9,
        out_specs=(in_vmem, in_vmem),
        scratch_shapes=[
            pltpu.VMEM((owned, rows, cols), f32),
            pltpu.VMEM((NVAR, rows, cols), f32),
            pltpu.VMEM((owned, NVAR, rows, cols), bf16),
            pltpu.VMEM((rows, cols), i32),
            pltpu.VMEM(folded, i32),
            pltpu.VMEM(folded, f32),
            pltpu.VMEM(folded, f32),
            pltpu.SMEM(coef_table.shape, f32),
            pltpu.SMEM(obs_counts.shape, i32),
            pltpu.VMEM((lane_tiles, deep, LANES), f32),
            pltpu.VMEM((lane_tiles, deep, LANES), f32),
            pltpu.VMEM((lane_tiles, rows, LANES), f32),
            *[pltpu.VMEM((owned + 1, lane_tiles, deep, LANES), f32)] * (STEPS + 1),
            *[pltpu.VMEM((fields, lane_tiles, deep, LANES), f32)] * (STEPS + 1),
            *message(owned + 1),
            *message(1),
            *message(NVAR),
            *message(owned),
            pltpu.VMEM((field_rows, WIDE), f32),
            pltpu.VMEM((2, field_rows, WIDE), bf16),
            pltpu.VMEM((WIDE, slots * LANES), bf16),
            pltpu.VMEM((field_rows, slots * LANES), bf16),
            pltpu.VMEM(folded, f32),
            pltpu.VMEM((4, half, LANES), f32),
            pltpu.VMEM((depth, half, LANES), f32),
            pltpu.VMEM(folded, f32),
            dma((9,)),
            dma((2, 2)),
            dma((2, 2)),
            dma((2, 2)),
            dma((2, 2)),
            dma((2, 4)),
            dma((2, depth)),
            dma((2,)),
        ],
        compiler_params=pltpu.CompilerParams(collective_id=0, has_side_effects=True, vmem_limit_bytes=48 * 2**20),
    )(
        in_hbm(alpha_fields),
        in_hbm(static_control),
        in_hbm(perturbations),
        in_hbm(coef_table),
        in_hbm(coef_class),
        in_hbm(obs_cells.reshape(folded)),
        obs_counts,
        in_hbm(innovations.reshape(folded)),
        in_hbm(obs_weights.reshape(folded)),
    )
    return pl.pallas_call(
        write_out,
        out_shape=shapes,
        in_specs=[anywhere, anywhere],
        out_specs=(anywhere, anywhere),
        scratch_shapes=[dma((2,))],
        compiler_params=pltpu.CompilerParams(vmem_limit_bytes=2**20),
    )(*grads)


def solution(mesh):
    in_specs = (
        P("mem", "tile", None),
        P(None, "tile", None),
        P("mem", None, "tile", None),
        P(),
        P("tile", None),
        P("tile", None),
        P("tile"),
        P("tile", None),
        P("tile", None),
    )
    out_specs = (P("mem", "tile", None), P(None, "tile", None))
    run = functools.partial(body, mesh.shape["tile"], mesh.shape["mem"])
    return jax.shard_map(run, mesh=mesh, in_specs=in_specs, out_specs=out_specs, check_vma=False)
```

```python
import functools

import jax
import jax.numpy as jnp
from jax import lax
from jax.experimental import pallas as pl
from jax.experimental.pallas import tpu as pltpu
from jax.sharding import PartitionSpec as P

MESH = pl.DeviceIdType.MESH
STEPS = 4
NVAR = 4
PAD = 8
LANES = 128
WIDE = 256
CHUNK = 2048


def advance(source, target, kappa, keep, f, starts):
    tiles = source.shape[1]
    lane = lax.broadcasted_iota(jnp.int32, (8, LANES), 1)
    first, last = lane == 0, lane == LANES - 1
    for r in starts:
        here = [source[f, j, pl.ds(r, 8), :] for j in range(tiles)]
        right = [pltpu.roll(a, 1, 1) for a in here]
        left = [pltpu.roll(a, LANES - 1, 1) for a in here]
        for j in range(tiles):
            before = jnp.where(first, right[j - 1] if j else 0.0, right[j])
            after = jnp.where(last, left[j + 1] if j < tiles - 1 else 0.0, left[j])
            around = (source[f, j, pl.ds(r - 1, 8), :] + source[f, j, pl.ds(r + 1, 8), :]) + (before + after)
            target[f, j, pl.ds(r, 8), :] = keep[j, pl.ds(r, 8), :] * here[j] + kappa[j, pl.ds(r, 8), :] * around


def inner_rows(stages, kappa, keep, f, rows):
    for s in range(STEPS):
        advance(stages[s], stages[s + 1], kappa, keep, f, range(PAD, PAD + rows, 8))


def border_rows(stages, kappa, keep, fields, rows):
    tiles = kappa.shape[0]
    lane = lax.broadcasted_iota(jnp.int32, (8, LANES), 1)
    first, last = lane == 0, lane == LANES - 1
    upper = lax.broadcasted_iota(jnp.int32, (8, LANES), 0) < 4
    for s in range(STEPS):
        top, bottom = PAD - 3 + s, PAD + rows - 1 - s

        def both(ref, index, shift):
            return jnp.where(upper, ref[(*index, pl.ds(top + shift, 8))], ref[(*index, pl.ds(bottom - 4 + shift, 8))])

        factor = [both(kappa, (j,), 0) for j in range(tiles)]
        kept = [both(keep, (j,), 0) for j in range(tiles)]
        source, target = stages[s], stages[s + 1]
        for f in fields:
            here = [both(source, (f, j), 0) for j in range(tiles)]
            right = [pltpu.roll(a, 1, 1) for a in here]
            left = [pltpu.roll(a, LANES - 1, 1) for a in here]
            for j in range(tiles):
                before = jnp.where(first, right[j - 1] if j else 0.0, right[j])
                after = jnp.where(last, left[j + 1] if j < tiles - 1 else 0.0, left[j])
                around = (both(source, (f, j), -1) + both(source, (f, j), 1)) + (before + after)
                value = kept[j] * here[j] + factor[j] * around
                target[f, j, pl.ds(top, 4), :] = value[:4]
                target[f, j, pl.ds(bottom, 4), :] = value[4:]


def kernel(
    tiles,
    members,
    alpha_hbm,
    static_hbm,
    pert_hbm,
    table_hbm,
    class_hbm,
    cells_hbm,
    counts_hbm,
    innov_hbm,
    weights_hbm,
    out_alpha,
    out_static,
    alpha,
    static,
    pert,
    classes,
    cells,
    innov,
    weights,
    table,
    counts,
    kappa,
    keep,
    inverse,
    fwd0,
    fwd1,
    fwd2,
    fwd3,
    fwd4,
    adj0,
    adj1,
    adj2,
    adj3,
    adj4,
    fwd_send,
    fwd_recv,
    static_send,
    static_recv,
    wide_send,
    wide_recv,
    adj_send,
    adj_recv,
    field,
    split,
    hot_lane,
    hot_row,
    obs,
    pair_buf,
    ring_buf,
    resid,
    in_sem,
    fwd_sems,
    static_sems,
    wide_sems,
    adj_sems,
    pair_sems,
    ring_sems,
    swap_sems,
):
    owned, rows, cols = alpha.shape
    lane_tiles = cols // LANES
    folds = cols // WIDE
    field_rows = NVAR * rows
    depth = members // 4
    slots = cells.shape[0]
    half = slots // 2
    scale = (owned * members - 1.0) ** (-0.5)
    fwd = (fwd0, fwd1, fwd2, fwd3, fwd4)
    adj = (adj0, adj1, adj2, adj3, adj4)
    m = lax.axis_index("mem")
    t = lax.axis_index("tile")
    core = lax.rem(m, 2)
    quad = lax.rem(m, 4)
    far = quad // 2
    level = m // 4
    stride = members // NVAR
    owner = lax.rem(m, stride) == stride // 2
    var = m // stride
    has_up = t > 0
    has_down = t < tiles - 1

    core_mate = m + 1 - 2 * core
    far_mate = m + 2 - 4 * far
    both_mate = core_mate + 2 - 4 * far

    barrier = pltpu.get_barrier_semaphore()

    @pl.when(has_up)
    def _():
        pl.semaphore_signal(barrier, inc=1, device_id={"tile": t - 1}, device_id_type=MESH)

    @pl.when(has_down)
    def _():
        pl.semaphore_signal(barrier, inc=1, device_id={"tile": t + 1}, device_id_type=MESH)

    loads = [
        pltpu.make_async_copy(class_hbm, classes, in_sem.at[0]),
        pltpu.make_async_copy(table_hbm, table, in_sem.at[1]),
        pltpu.make_async_copy(alpha_hbm, alpha, in_sem.at[2]),
        pltpu.make_async_copy(static_hbm, static, in_sem.at[3]),
        pltpu.make_async_copy(cells_hbm, cells, in_sem.at[4]),
        pltpu.make_async_copy(counts_hbm, counts, in_sem.at[5]),
        pltpu.make_async_copy(innov_hbm, innov, in_sem.at[6]),
        pltpu.make_async_copy(weights_hbm, weights, in_sem.at[7]),
        pltpu.make_async_copy(pert_hbm, pert, in_sem.at[8]),
    ]
    for i in (0, 1, 2, 4, 3, 5, 6, 7, 8):
        loads[i].start()

    for mate in (core_mate, far_mate, both_mate):
        pl.semaphore_signal(barrier, inc=1, device_id={"mem": mate}, device_id_type=MESH)
    for d in range(1, depth):
        mate = lax.rem(level + d, depth) * 4 + quad
        pl.semaphore_signal(barrier, inc=1, device_id={"mem": mate}, device_id_type=MESH)

    for edge, missing in ((0, t == 0), (1, t == tiles - 1)):

        @pl.when(missing)
        def _():
            fwd_recv[edge] = jnp.zeros(fwd_recv.shape[1:], jnp.float32)
            static_recv[edge] = jnp.zeros(static_recv.shape[1:], jnp.float32)
            wide_recv[edge] = jnp.zeros(wide_recv.shape[1:], jnp.float32)
            adj_recv[edge] = jnp.zeros(adj_recv.shape[1:], jnp.float32)

    def exchange(send, recv, sems):
        up = pltpu.make_async_remote_copy(
            send.at[0], recv.at[1], sems.at[0, 0], sems.at[1, 1], device_id={"tile": t - 1}, device_id_type=MESH
        )
        down = pltpu.make_async_remote_copy(
            send.at[1], recv.at[0], sems.at[0, 1], sems.at[1, 0], device_id={"tile": t + 1}, device_id_type=MESH
        )
        return up, down

    def start(pair):
        @pl.when(has_up)
        def _():
            pair[0].start()

        @pl.when(has_down)
        def _():
            pair[1].start()

    def wait(pair):
        @pl.when(has_up)
        def _():
            pair[0].wait_send()
            pair[1].wait_recv()

        @pl.when(has_down)
        def _():
            pair[1].wait_send()
            pair[0].wait_recv()

    def pack(send, g, top, bottom):
        at = pl.ds(4 * (g % 2), STEPS)
        send[0, g // 2, at, :] = top
        send[1, g // 2, at, :] = bottom

    def unpack(recv, g, target, index):
        at = pl.ds(4 * (g % 2), STEPS)
        target[(*index, pl.ds(PAD - STEPS, STEPS), slice(None))] = recv[0, g // 2, at, :]
        target[(*index, pl.ds(PAD + rows, STEPS), slice(None))] = recv[1, g // 2, at, :]

    own = pl.ds(PAD, rows)
    top_rows = pl.ds(PAD, STEPS)
    bottom_rows = pl.ds(PAD + rows - STEPS, STEPS)
    columns = [pl.ds(j * LANES, LANES) for j in range(lane_tiles)]

    loads[0].wait()
    loads[1].wait()
    for j in range(lane_tiles):
        kind = classes[:, columns[j]]
        value = jnp.full(kind.shape, table[0], jnp.float32)
        for i in range(1, table.shape[0]):
            value = jnp.where(kind == i, table[i], value)
        kappa[j, own, :] = value
        keep[j, own, :] = 1.0 - 4.0 * value
        pack(fwd_send, owned * lane_tiles + j, value[:STEPS], value[rows - STEPS :])
    loads[2].wait()
    for f in range(owned):
        for j in range(lane_tiles):
            fwd0[f, j, own, :] = alpha[f, :, columns[j]]
            pack(fwd_send, f * lane_tiles + j, fwd0[f, j, top_rows, :], fwd0[f, j, bottom_rows, :])
    pl.semaphore_wait(barrier, depth + 2 + has_up.astype(jnp.int32) + has_down.astype(jnp.int32))
    fwd_pair = exchange(fwd_send, fwd_recv, fwd_sems)
    start(fwd_pair)
    static_pair = exchange(static_send, static_recv, static_sems)
    loads[3].wait()

    @pl.when(owner)
    def _():
        for j in range(lane_tiles):
            fwd0[owned, j, own, :] = static[var, :, columns[j]]
            pack(static_send, j, fwd0[owned, j, top_rows, :], fwd0[owned, j, bottom_rows, :])
        start(static_pair)

    loads[4].wait()
    lane_of = lax.broadcasted_iota(jnp.int32, (WIDE, LANES), 0)
    three_rows = folds * lax.broadcasted_iota(jnp.int32, (field_rows, LANES), 0)

    def make_hot_lane(i, carry):
        at = pl.ds(pl.multiple_of(i * LANES, LANES), LANES)
        hot_lane[:, at] = jnp.where(lane_of == (cells[pl.ds(i, 1), :] & (WIDE - 1)), 1.0, 0.0).astype(jnp.bfloat16)
        return carry

    def make_hot_row(i, carry):
        at = pl.ds(pl.multiple_of(i * LANES, LANES), LANES)
        row = cells[pl.ds(i, 1), :] // WIDE
        for fold in range(folds):
            hot = jnp.where(three_rows == row - fold, 1.0, 0.0).astype(jnp.bfloat16)
            hot_row[pl.ds(fold * field_rows, field_rows), at] = hot
        return carry

    lax.fori_loop(0, slots, make_hot_lane, 0)

    def inner_fwd(f, carry):
        inner_rows(fwd, kappa, keep, f, rows)
        return carry

    lax.fori_loop(0, owned, inner_fwd, 0)

    @pl.when(owner)
    def _():
        inner_rows(fwd, kappa, keep, owned, rows)

    for load in loads[5:]:
        load.wait()

    wait(fwd_pair)
    for j in range(lane_tiles):
        unpack(fwd_recv, owned * lane_tiles + j, kappa, (j,))
        for at in (pl.ds(PAD - STEPS, STEPS), pl.ds(PAD + rows, STEPS)):
            keep[j, at, :] = 1.0 - 4.0 * kappa[j, at, :]
        for f in range(owned):
            unpack(fwd_recv, f * lane_tiles + j, fwd0, (f, j))
    border_rows(fwd, kappa, keep, range(owned), rows)

    def place(v, j):
        return pl.ds((j * LANES // WIDE) * field_rows + v * rows, rows), pl.ds(j * LANES % WIDE, LANES)

    for j in range(lane_tiles):
        for v in range(NVAR):
            total = pert[0, v, :, columns[j]].astype(jnp.float32) * fwd4[0, j, own, :]
            for f in range(1, owned):
                total = total + pert[f, v, :, columns[j]].astype(jnp.float32) * fwd4[f, j, own, :]
            field[place(v, j)] = scale * total

    @pl.when(owner)
    def _():
        wait(static_pair)
        for j in range(lane_tiles):
            unpack(static_recv, j, fwd0, (owned, j))
        border_rows(fwd, kappa, keep, (owned,), rows)
        for j in range(lane_tiles):
            at = place(0, j)
            at = (pl.ds(pl.multiple_of(at[0].start + var * rows, rows), rows), at[1])
            field[at] = field[at] + fwd4[owned, j, own, :]

    high = field[...].astype(jnp.bfloat16)
    split[0] = high
    split[1] = (field[...] - high.astype(jnp.float32)).astype(jnp.bfloat16)

    per_chunk = CHUNK // LANES
    row_chunk = folds * lax.broadcasted_iota(jnp.int32, (field_rows, CHUNK), 0)

    def pick(i, carry):
        at = pl.ds(pl.multiple_of(i * CHUNK, CHUNK), CHUNK)
        hot = hot_lane[:, at]
        found = jnp.dot(split[0], hot, preferred_element_type=jnp.float32)
        found = found + jnp.dot(split[1], hot, preferred_element_type=jnp.float32)
        row = jnp.concatenate([cells[pl.ds(per_chunk * i + q, 1), :] for q in range(per_chunk)], 1) // WIDE
        kept = jnp.zeros((field_rows, CHUNK), jnp.float32)
        for fold in range(folds):
            kept = jnp.where(row_chunk == row - fold, found[fold * field_rows : (fold + 1) * field_rows], kept)
        value = jnp.sum(kept, 0, keepdims=True)
        for q in range(per_chunk):
            obs[pl.ds(per_chunk * i + q, 1), :] = value[:, q * LANES : (q + 1) * LANES]
        return carry

    mine = pl.ds(pl.multiple_of(core * half, 8), half)
    others = pl.ds(pl.multiple_of((1 - core) * half, 8), half)
    blocks = half // per_chunk

    def pair_copy(source, mate, sender, at):
        return pltpu.make_async_remote_copy(
            source, pair_buf.at[sender], pair_sems.at[0, at], pair_sems.at[1, sender], device_id={"mem": mate}, device_id_type=MESH
        )

    lax.fori_loop((1 - core) * blocks, (2 - core) * blocks, pick, 0)
    pair_both = pair_copy(obs.at[others], both_mate, quad, 1)
    pair_core = pair_copy(obs.at[others], core_mate, quad, 0)
    pair_both.start()
    pair_core.start()
    lax.fori_loop(core * blocks, (core + 1) * blocks, pick, 0)
    pair_far = pair_copy(obs.at[mine], far_mate, quad, 2)
    pair_far.start()
    pair_buf[quad] = obs[mine]
    for mate in (core_mate, far_mate, both_mate):
        pair_copy(obs.at[mine], mate, lax.rem(mate, 4), 0).wait_recv()
    ring_buf[level] = pair_buf[0] + pair_buf[1] + pair_buf[2] + pair_buf[3]

    def ring_copy(d):
        to = lax.rem(level + d, depth) * 4 + quad
        return pltpu.make_async_remote_copy(
            ring_buf.at[level], ring_buf.at[level], ring_sems.at[0, d], ring_sems.at[1, level], device_id={"mem": to}, device_id_type=MESH
        )

    order = sorted(range(1, depth), key=lambda d: -min(d, depth - d))
    for d in order:
        ring_copy(d).start()
    lax.fori_loop(0, slots, make_hot_row, 0)
    for j in range(lane_tiles):
        inverse[j] = 1.0 / kappa[j, own, :]
    for d in range(1, depth):
        other = lax.rem(level + d, depth)
        pltpu.make_async_remote_copy(
            ring_buf.at[other],
            ring_buf.at[other],
            ring_sems.at[0, d],
            ring_sems.at[1, other],
            device_id={"mem": other * 4 + quad},
            device_id_type=MESH,
        ).wait_recv()
    observed = ring_buf[0]
    for d in range(1, depth):
        observed = observed + ring_buf[d]
    slot = lax.broadcasted_iota(jnp.int32, (half, LANES), 0) * LANES + lax.broadcasted_iota(jnp.int32, (half, LANES), 1)
    slot = slot + core * (half * LANES)
    resid[mine] = jnp.where(slot < counts[0], (observed - innov[mine]) * weights[mine], 0.0)
    swap = pltpu.make_async_remote_copy(
        resid.at[mine], resid.at[mine], swap_sems.at[0], swap_sems.at[1], device_id={"mem": core_mate}, device_id_type=MESH
    )
    swap.start()

    def spread(which):
        at = pl.ds(pl.multiple_of(which * (half * LANES), half * LANES), half * LANES)
        value = jnp.concatenate([resid[pl.ds(which * half + q, 1), :] for q in range(half)], 1)
        high = value.astype(jnp.bfloat16)
        low = (value - high.astype(jnp.float32)).astype(jnp.bfloat16)
        hot = hot_lane[:, at]
        row = hot_row[:, at]
        return lax.dot_general(
            jnp.concatenate([row, row], 1),
            jnp.concatenate([hot * high, hot * low], 1),
            (((1,), (1,)), ((), ())),
            preferred_element_type=jnp.float32,
        )

    field[...] = spread(core)
    swap.wait()
    field[...] = field[...] + spread(1 - core)

    for j in range(lane_tiles):
        for v in range(NVAR):
            adj0[owned + v, j, own, :] = kappa[j, own, :] * field[place(v, j)]
            pack(wide_send, v * lane_tiles + j, adj0[owned + v, j, top_rows, :], adj0[owned + v, j, bottom_rows, :])
    wide_pair = exchange(wide_send, wide_recv, wide_sems)
    start(wide_pair)
    for j in range(lane_tiles):
        for f in range(owned):
            total = pert[f, 0, :, columns[j]].astype(jnp.float32) * field[place(0, j)]
            for v in range(1, NVAR):
                total = total + pert[f, v, :, columns[j]].astype(jnp.float32) * field[place(v, j)]
            adj0[f, j, own, :] = kappa[j, own, :] * (scale * total)
            pack(adj_send, f * lane_tiles + j, adj0[f, j, top_rows, :], adj0[f, j, bottom_rows, :])
    adj_pair = exchange(adj_send, adj_recv, adj_sems)
    start(adj_pair)

    def inner_adj(f, carry):
        inner_rows(adj, kappa, keep, f, rows)
        return carry

    lax.fori_loop(0, owned + NVAR, inner_adj, 0)
    pair_core.wait_send()
    pair_both.wait_send()
    pair_far.wait_send()
    for d in range(1, depth):
        ring_copy(d).wait_send()
    wait(wide_pair)
    for j in range(lane_tiles):
        for v in range(NVAR):
            unpack(wide_recv, v * lane_tiles + j, adj0, (owned + v, j))
    border_rows(adj, kappa, keep, range(owned, owned + NVAR), rows)
    for j in range(lane_tiles):
        for v in range(NVAR):
            out_static[v, :, columns[j]] = static[v, :, columns[j]] + adj4[owned + v, j, own, :] * inverse[j]
    wait(adj_pair)
    for j in range(lane_tiles):
        for f in range(owned):
            unpack(adj_recv, f * lane_tiles + j, adj0, (f, j))
    border_rows(adj, kappa, keep, range(owned), rows)
    for j in range(lane_tiles):
        for f in range(owned):
            out_alpha[f, :, columns[j]] = alpha[f, :, columns[j]] + adj4[f, j, own, :] * inverse[j]


def write_out(alpha, static, out_alpha, out_static, sems):
    copies = [pltpu.make_async_copy(alpha, out_alpha, sems.at[0]), pltpu.make_async_copy(static, out_static, sems.at[1])]
    for copy in copies:
        copy.start()
    for copy in copies:
        copy.wait()


def body(tiles, members, alpha_fields, static_control, perturbations, coef_table, coef_class, obs_cells, obs_counts, innovations, obs_weights):
    owned, rows, cols = alpha_fields.shape
    slots = obs_cells.shape[1] // LANES
    folded = (slots, LANES)
    half = slots // 2
    depth = members // 4
    fields = owned + NVAR
    lane_tiles = cols // LANES
    deep = rows + 2 * PAD
    field_rows = cols // WIDE * NVAR * rows
    f32, bf16, i32 = jnp.float32, jnp.bfloat16, jnp.int32
    anywhere = pl.BlockSpec(memory_space=pl.ANY)
    in_hbm = functools.partial(pltpu.with_memory_space_constraint, memory_space=pltpu.HBM)
    in_vmem = pl.BlockSpec(memory_space=pltpu.VMEM)
    dma = pltpu.SemaphoreType.DMA

    def message(count):
        return [pltpu.VMEM((2, count * lane_tiles // 2, 8, LANES), f32)] * 2

    shapes = (jax.ShapeDtypeStruct((owned, rows, cols), f32), jax.ShapeDtypeStruct((NVAR, rows, cols), f32))
    grads = pl.pallas_call(
        functools.partial(kernel, tiles, members),
        out_shape=shapes,
        in_specs=[anywhere] * 9,
        out_specs=(in_vmem, in_vmem),
        scratch_shapes=[
            pltpu.VMEM((owned, rows, cols), f32),
            pltpu.VMEM((NVAR, rows, cols), f32),
            pltpu.VMEM((owned, NVAR, rows, cols), bf16),
            pltpu.VMEM((rows, cols), i32),
            pltpu.VMEM(folded, i32),
            pltpu.VMEM(folded, f32),
            pltpu.VMEM(folded, f32),
            pltpu.SMEM(coef_table.shape, f32),
            pltpu.SMEM(obs_counts.shape, i32),
            pltpu.VMEM((lane_tiles, deep, LANES), f32),
            pltpu.VMEM((lane_tiles, deep, LANES), f32),
            pltpu.VMEM((lane_tiles, rows, LANES), f32),
            *[pltpu.VMEM((owned + 1, lane_tiles, deep, LANES), f32)] * (STEPS + 1),
            *[pltpu.VMEM((fields, lane_tiles, deep, LANES), f32)] * (STEPS + 1),
            *message(owned + 1),
            *message(1),
            *message(NVAR),
            *message(owned),
            pltpu.VMEM((field_rows, WIDE), f32),
            pltpu.VMEM((2, field_rows, WIDE), bf16),
            pltpu.VMEM((WIDE, slots * LANES), bf16),
            pltpu.VMEM((field_rows, slots * LANES), bf16),
            pltpu.VMEM(folded, f32),
            pltpu.VMEM((4, half, LANES), f32),
            pltpu.VMEM((depth, half, LANES), f32),
            pltpu.VMEM(folded, f32),
            dma((9,)),
            dma((2, 2)),
            dma((2, 2)),
            dma((2, 2)),
            dma((2, 2)),
            dma((2, 4)),
            dma((2, depth)),
            dma((2,)),
        ],
        compiler_params=pltpu.CompilerParams(collective_id=0, has_side_effects=True, vmem_limit_bytes=48 * 2**20),
    )(
        in_hbm(alpha_fields),
        in_hbm(static_control),
        in_hbm(perturbations),
        in_hbm(coef_table),
        in_hbm(coef_class),
        in_hbm(obs_cells.reshape(folded)),
        obs_counts,
        in_hbm(innovations.reshape(folded)),
        in_hbm(obs_weights.reshape(folded)),
    )
    return pl.pallas_call(
        write_out,
        out_shape=shapes,
        in_specs=[anywhere, anywhere],
        out_specs=(anywhere, anywhere),
        scratch_shapes=[dma((2,))],
        compiler_params=pltpu.CompilerParams(vmem_limit_bytes=2**20),
    )(*grads)


def solution(mesh):
    in_specs = (
        P("mem", "tile", None),
        P(None, "tile", None),
        P("mem", None, "tile", None),
        P(),
        P("tile", None),
        P("tile", None),
        P("tile"),
        P("tile", None),
        P("tile", None),
    )
    out_specs = (P("mem", "tile", None), P(None, "tile", None))
    run = functools.partial(body, mesh.shape["tile"], mesh.shape["mem"])
    return jax.shard_map(run, mesh=mesh, in_specs=in_specs, out_specs=out_specs, check_vma=False)
```

```python
import functools

import jax
import jax.numpy as jnp
from jax import lax
from jax.experimental import pallas as pl
from jax.experimental.pallas import tpu as pltpu
from jax.sharding import PartitionSpec as P

MESH = pl.DeviceIdType.MESH
STEPS = 4
NVAR = 4
PAD = 8
LANES = 128
WIDE = 256
CHUNK = 2048


def advance(source, target, kappa, keep, f, starts):
    tiles = source.shape[1]
    lane = lax.broadcasted_iota(jnp.int32, (8, LANES), 1)
    first, last = lane == 0, lane == LANES - 1
    for r in starts:
        here = [source[f, j, pl.ds(r, 8), :] for j in range(tiles)]
        right = [pltpu.roll(a, 1, 1) for a in here]
        left = [pltpu.roll(a, LANES - 1, 1) for a in here]
        for j in range(tiles):
            before = jnp.where(first, right[j - 1] if j else 0.0, right[j])
            after = jnp.where(last, left[j + 1] if j < tiles - 1 else 0.0, left[j])
            around = (source[f, j, pl.ds(r - 1, 8), :] + source[f, j, pl.ds(r + 1, 8), :]) + (before + after)
            target[f, j, pl.ds(r, 8), :] = keep[j, pl.ds(r, 8), :] * here[j] + kappa[j, pl.ds(r, 8), :] * around


def inner_rows(stages, kappa, keep, f, rows):
    for s in range(STEPS):
        advance(stages[s], stages[s + 1], kappa, keep, f, range(PAD, PAD + rows, 8))


def border_rows(stages, kappa, keep, fields, rows):
    tiles = kappa.shape[0]
    lane = lax.broadcasted_iota(jnp.int32, (8, LANES), 1)
    first, last = lane == 0, lane == LANES - 1
    upper = lax.broadcasted_iota(jnp.int32, (8, LANES), 0) < 4
    for s in range(STEPS):
        top, bottom = PAD - 3 + s, PAD + rows - 1 - s

        def both(ref, index, shift):
            return jnp.where(upper, ref[(*index, pl.ds(top + shift, 8))], ref[(*index, pl.ds(bottom - 4 + shift, 8))])

        factor = [both(kappa, (j,), 0) for j in range(tiles)]
        kept = [both(keep, (j,), 0) for j in range(tiles)]
        source, target = stages[s], stages[s + 1]
        for f in fields:
            here = [both(source, (f, j), 0) for j in range(tiles)]
            right = [pltpu.roll(a, 1, 1) for a in here]
            left = [pltpu.roll(a, LANES - 1, 1) for a in here]
            for j in range(tiles):
                before = jnp.where(first, right[j - 1] if j else 0.0, right[j])
                after = jnp.where(last, left[j + 1] if j < tiles - 1 else 0.0, left[j])
                around = (both(source, (f, j), -1) + both(source, (f, j), 1)) + (before + after)
                value = kept[j] * here[j] + factor[j] * around
                target[f, j, pl.ds(top, 4), :] = value[:4]
                target[f, j, pl.ds(bottom, 4), :] = value[4:]


def kernel(
    tiles,
    members,
    alpha_hbm,
    static_hbm,
    pert_hbm,
    table_hbm,
    class_hbm,
    cells_hbm,
    counts_hbm,
    innov_hbm,
    weights_hbm,
    out_alpha,
    out_static,
    alpha,
    static,
    pert,
    classes,
    cells,
    innov,
    weights,
    table,
    counts,
    kappa,
    keep,
    inverse,
    fwd0,
    fwd1,
    fwd2,
    fwd3,
    fwd4,
    adj0,
    adj1,
    adj2,
    adj3,
    adj4,
    fwd_send,
    fwd_recv,
    static_send,
    static_recv,
    wide_send,
    wide_recv,
    adj_send,
    adj_recv,
    field,
    split,
    hot_lane,
    hot_row,
    obs,
    pair_buf,
    ring_buf,
    resid,
    in_sem,
    fwd_sems,
    static_sems,
    wide_sems,
    adj_sems,
    pair_sems,
    ring_sems,
    swap_sems,
):
    owned, rows, cols = alpha.shape
    lane_tiles = cols // LANES
    folds = cols // WIDE
    field_rows = NVAR * rows
    depth = members // 4
    slots = cells.shape[0]
    half = slots // 2
    scale = (owned * members - 1.0) ** (-0.5)
    fwd = (fwd0, fwd1, fwd2, fwd3, fwd4)
    adj = (adj0, adj1, adj2, adj3, adj4)
    m = lax.axis_index("mem")
    t = lax.axis_index("tile")
    core = lax.rem(m, 2)
    quad = lax.rem(m, 4)
    far = quad // 2
    level = m // 4
    stride = members // NVAR
    owner = lax.rem(m, stride) == stride // 2
    var = m // stride
    has_up = t > 0
    has_down = t < tiles - 1

    core_mate = m + 1 - 2 * core
    far_mate = m + 2 - 4 * far
    both_mate = core_mate + 2 - 4 * far

    barrier = pltpu.get_barrier_semaphore()

    @pl.when(has_up)
    def _():
        pl.semaphore_signal(barrier, inc=1, device_id={"tile": t - 1}, device_id_type=MESH)

    @pl.when(has_down)
    def _():
        pl.semaphore_signal(barrier, inc=1, device_id={"tile": t + 1}, device_id_type=MESH)

    loads = [
        pltpu.make_async_copy(class_hbm, classes, in_sem.at[0]),
        pltpu.make_async_copy(table_hbm, table, in_sem.at[1]),
        pltpu.make_async_copy(alpha_hbm, alpha, in_sem.at[2]),
        pltpu.make_async_copy(static_hbm, static, in_sem.at[3]),
        pltpu.make_async_copy(cells_hbm, cells, in_sem.at[4]),
        pltpu.make_async_copy(counts_hbm, counts, in_sem.at[5]),
        pltpu.make_async_copy(innov_hbm, innov, in_sem.at[6]),
        pltpu.make_async_copy(weights_hbm, weights, in_sem.at[7]),
        pltpu.make_async_copy(pert_hbm, pert, in_sem.at[8]),
    ]
    for i in (0, 1, 2, 4, 3, 5, 6, 7, 8):
        loads[i].start()

    for mate in (core_mate, far_mate, both_mate):
        pl.semaphore_signal(barrier, inc=1, device_id={"mem": mate}, device_id_type=MESH)
    for d in range(1, depth):
        mate = lax.rem(level + d, depth) * 4 + quad
        pl.semaphore_signal(barrier, inc=1, device_id={"mem": mate}, device_id_type=MESH)

    for edge, missing in ((0, t == 0), (1, t == tiles - 1)):

        @pl.when(missing)
        def _():
            fwd_recv[edge] = jnp.zeros(fwd_recv.shape[1:], jnp.float32)
            static_recv[edge] = jnp.zeros(static_recv.shape[1:], jnp.float32)
            wide_recv[edge] = jnp.zeros(wide_recv.shape[1:], jnp.float32)
            adj_recv[edge] = jnp.zeros(adj_recv.shape[1:], jnp.float32)

    def exchange(send, recv, sems):
        up = pltpu.make_async_remote_copy(
            send.at[0], recv.at[1], sems.at[0, 0], sems.at[1, 1], device_id={"tile": t - 1}, device_id_type=MESH
        )
        down = pltpu.make_async_remote_copy(
            send.at[1], recv.at[0], sems.at[0, 1], sems.at[1, 0], device_id={"tile": t + 1}, device_id_type=MESH
        )
        return up, down

    def start(pair):
        @pl.when(has_up)
        def _():
            pair[0].start()

        @pl.when(has_down)
        def _():
            pair[1].start()

    def wait(pair):
        @pl.when(has_up)
        def _():
            pair[0].wait_send()
            pair[1].wait_recv()

        @pl.when(has_down)
        def _():
            pair[1].wait_send()
            pair[0].wait_recv()

    def pack(send, g, top, bottom):
        at = pl.ds(4 * (g % 2), STEPS)
        send[0, g // 2, at, :] = top
        send[1, g // 2, at, :] = bottom

    def unpack(recv, g, target, index):
        at = pl.ds(4 * (g % 2), STEPS)
        target[(*index, pl.ds(PAD - STEPS, STEPS), slice(None))] = recv[0, g // 2, at, :]
        target[(*index, pl.ds(PAD + rows, STEPS), slice(None))] = recv[1, g // 2, at, :]

    own = pl.ds(PAD, rows)
    top_rows = pl.ds(PAD, STEPS)
    bottom_rows = pl.ds(PAD + rows - STEPS, STEPS)
    columns = [pl.ds(j * LANES, LANES) for j in range(lane_tiles)]

    loads[0].wait()
    loads[1].wait()
    for j in range(lane_tiles):
        kind = classes[:, columns[j]]
        value = jnp.full(kind.shape, table[0], jnp.float32)
        for i in range(1, table.shape[0]):
            value = jnp.where(kind == i, table[i], value)
        kappa[j, own, :] = value
        keep[j, own, :] = 1.0 - 4.0 * value
        pack(fwd_send, owned * lane_tiles + j, value[:STEPS], value[rows - STEPS :])
    loads[2].wait()
    for f in range(owned):
        for j in range(lane_tiles):
            fwd0[f, j, own, :] = alpha[f, :, columns[j]]
            pack(fwd_send, f * lane_tiles + j, fwd0[f, j, top_rows, :], fwd0[f, j, bottom_rows, :])
    pl.semaphore_wait(barrier, depth + 2 + has_up.astype(jnp.int32) + has_down.astype(jnp.int32))
    fwd_pair = exchange(fwd_send, fwd_recv, fwd_sems)
    start(fwd_pair)
    static_pair = exchange(static_send, static_recv, static_sems)
    loads[3].wait()

    @pl.when(owner)
    def _():
        for j in range(lane_tiles):
            fwd0[owned, j, own, :] = static[var, :, columns[j]]
            pack(static_send, j, fwd0[owned, j, top_rows, :], fwd0[owned, j, bottom_rows, :])
        start(static_pair)

    loads[4].wait()
    lane_of = lax.broadcasted_iota(jnp.int32, (WIDE, LANES), 0)
    three_rows = folds * lax.broadcasted_iota(jnp.int32, (field_rows, LANES), 0)

    def make_hot_lane(i, carry):
        at = pl.ds(pl.multiple_of(i * LANES, LANES), LANES)
        hot_lane[:, at] = jnp.where(lane_of == (cells[pl.ds(i, 1), :] & (WIDE - 1)), 1.0, 0.0).astype(jnp.bfloat16)
        return carry

    def make_hot_row(i, carry):
        at = pl.ds(pl.multiple_of(i * LANES, LANES), LANES)
        row = cells[pl.ds(i, 1), :] // WIDE
        for fold in range(folds):
            hot = jnp.where(three_rows == row - fold, 1.0, 0.0).astype(jnp.bfloat16)
            hot_row[pl.ds(fold * field_rows, field_rows), at] = hot
        return carry

    lax.fori_loop(0, slots, make_hot_lane, 0)

    def inner_fwd(f, carry):
        inner_rows(fwd, kappa, keep, f, rows)
        return carry

    lax.fori_loop(0, owned, inner_fwd, 0)

    @pl.when(owner)
    def _():
        inner_rows(fwd, kappa, keep, owned, rows)

    for load in loads[5:]:
        load.wait()

    wait(fwd_pair)
    for j in range(lane_tiles):
        unpack(fwd_recv, owned * lane_tiles + j, kappa, (j,))
        for at in (pl.ds(PAD - STEPS, STEPS), pl.ds(PAD + rows, STEPS)):
            keep[j, at, :] = 1.0 - 4.0 * kappa[j, at, :]
        for f in range(owned):
            unpack(fwd_recv, f * lane_tiles + j, fwd0, (f, j))
    border_rows(fwd, kappa, keep, range(owned), rows)

    def place(v, j):
        return pl.ds((j * LANES // WIDE) * field_rows + v * rows, rows), pl.ds(j * LANES % WIDE, LANES)

    for j in range(lane_tiles):
        for v in range(NVAR):
            total = pert[0, v, :, columns[j]].astype(jnp.float32) * fwd4[0, j, own, :]
            for f in range(1, owned):
                total = total + pert[f, v, :, columns[j]].astype(jnp.float32) * fwd4[f, j, own, :]
            field[place(v, j)] = scale * total

    @pl.when(owner)
    def _():
        wait(static_pair)
        for j in range(lane_tiles):
            unpack(static_recv, j, fwd0, (owned, j))
        border_rows(fwd, kappa, keep, (owned,), rows)
        for j in range(lane_tiles):
            at = place(0, j)
            at = (pl.ds(pl.multiple_of(at[0].start + var * rows, rows), rows), at[1])
            field[at] = field[at] + fwd4[owned, j, own, :]

    high = field[...].astype(jnp.bfloat16)
    split[0] = high
    split[1] = (field[...] - high.astype(jnp.float32)).astype(jnp.bfloat16)

    per_chunk = CHUNK // LANES
    row_chunk = folds * lax.broadcasted_iota(jnp.int32, (field_rows, CHUNK), 0)

    def pick(i, carry):
        at = pl.ds(pl.multiple_of(i * CHUNK, CHUNK), CHUNK)
        hot = hot_lane[:, at]
        found = jnp.dot(split[0], hot, preferred_element_type=jnp.float32)
        found = found + jnp.dot(split[1], hot, preferred_element_type=jnp.float32)
        row = jnp.concatenate([cells[pl.ds(per_chunk * i + q, 1), :] for q in range(per_chunk)], 1) // WIDE
        kept = jnp.zeros((field_rows, CHUNK), jnp.float32)
        for fold in range(folds):
            kept = jnp.where(row_chunk == row - fold, found[fold * field_rows : (fold + 1) * field_rows], kept)
        value = jnp.sum(kept, 0, keepdims=True)
        for q in range(per_chunk):
            obs[pl.ds(per_chunk * i + q, 1), :] = value[:, q * LANES : (q + 1) * LANES]
        return carry

    mine = pl.ds(pl.multiple_of(core * half, 8), half)
    others = pl.ds(pl.multiple_of((1 - core) * half, 8), half)
    blocks = half // per_chunk

    def pair_copy(source, mate, sender, at):
        return pltpu.make_async_remote_copy(
            source, pair_buf.at[sender], pair_sems.at[0, at], pair_sems.at[1, sender], device_id={"mem": mate}, device_id_type=MESH
        )

    lax.fori_loop((1 - core) * blocks, (2 - core) * blocks, pick, 0)
    pair_both = pair_copy(obs.at[others], both_mate, quad, 1)
    pair_core = pair_copy(obs.at[others], core_mate, quad, 0)
    pair_both.start()
    pair_core.start()
    lax.fori_loop(core * blocks, (core + 1) * blocks, pick, 0)
    pair_far = pair_copy(obs.at[mine], far_mate, quad, 2)
    pair_far.start()
    pair_buf[quad] = obs[mine]
    for mate in (core_mate, far_mate, both_mate):
        pair_copy(obs.at[mine], mate, lax.rem(mate, 4), 0).wait_recv()
    ring_buf[level] = pair_buf[0] + pair_buf[1] + pair_buf[2] + pair_buf[3]

    def ring_copy(d):
        to = lax.rem(level + d, depth) * 4 + quad
        return pltpu.make_async_remote_copy(
            ring_buf.at[level], ring_buf.at[level], ring_sems.at[0, d], ring_sems.at[1, level], device_id={"mem": to}, device_id_type=MESH
        )

    order = sorted(range(1, depth), key=lambda d: -min(d, depth - d))
    for d in order:
        ring_copy(d).start()
    lax.fori_loop(0, slots, make_hot_row, 0)
    for j in range(lane_tiles):
        inverse[j] = 1.0 / kappa[j, own, :]
    for d in range(1, depth):
        other = lax.rem(level + d, depth)
        pltpu.make_async_remote_copy(
            ring_buf.at[other],
            ring_buf.at[other],
            ring_sems.at[0, d],
            ring_sems.at[1, other],
            device_id={"mem": other * 4 + quad},
            device_id_type=MESH,
        ).wait_recv()
    observed = ring_buf[0]
    for d in range(1, depth):
        observed = observed + ring_buf[d]
    slot = lax.broadcasted_iota(jnp.int32, (half, LANES), 0) * LANES + lax.broadcasted_iota(jnp.int32, (half, LANES), 1)
    slot = slot + core * (half * LANES)
    resid[mine] = jnp.where(slot < counts[0], (observed - innov[mine]) * weights[mine], 0.0)
    swap = pltpu.make_async_remote_copy(
        resid.at[mine], resid.at[mine], swap_sems.at[0], swap_sems.at[1], device_id={"mem": core_mate}, device_id_type=MESH
    )
    swap.start()

    def spread(which):
        at = pl.ds(pl.multiple_of(which * (half * LANES), half * LANES), half * LANES)
        value = jnp.concatenate([resid[pl.ds(which * half + q, 1), :] for q in range(half)], 1)
        high = value.astype(jnp.bfloat16)
        low = (value - high.astype(jnp.float32)).astype(jnp.bfloat16)
        hot = hot_lane[:, at]
        row = hot_row[:, at]
        return lax.dot_general(
            jnp.concatenate([row, row], 1),
            jnp.concatenate([hot * high, hot * low], 1),
            (((1,), (1,)), ((), ())),
            preferred_element_type=jnp.float32,
        )

    field[...] = spread(core)
    swap.wait()
    field[...] = field[...] + spread(1 - core)

    for j in range(lane_tiles):
        for v in range(NVAR):
            adj0[owned + v, j, own, :] = kappa[j, own, :] * field[place(v, j)]
            pack(wide_send, v * lane_tiles + j, adj0[owned + v, j, top_rows, :], adj0[owned + v, j, bottom_rows, :])
    wide_pair = exchange(wide_send, wide_recv, wide_sems)
    start(wide_pair)
    for j in range(lane_tiles):
        for f in range(owned):
            total = pert[f, 0, :, columns[j]].astype(jnp.float32) * field[place(0, j)]
            for v in range(1, NVAR):
                total = total + pert[f, v, :, columns[j]].astype(jnp.float32) * field[place(v, j)]
            adj0[f, j, own, :] = kappa[j, own, :] * (scale * total)
            pack(adj_send, f * lane_tiles + j, adj0[f, j, top_rows, :], adj0[f, j, bottom_rows, :])
    adj_pair = exchange(adj_send, adj_recv, adj_sems)
    start(adj_pair)

    def inner_adj(f, carry):
        inner_rows(adj, kappa, keep, f, rows)
        return carry

    lax.fori_loop(0, owned + NVAR, inner_adj, 0)
    pair_core.wait_send()
    pair_both.wait_send()
    pair_far.wait_send()
    for d in range(1, depth):
        ring_copy(d).wait_send()
    wait(wide_pair)
    for j in range(lane_tiles):
        for v in range(NVAR):
            unpack(wide_recv, v * lane_tiles + j, adj0, (owned + v, j))
    border_rows(adj, kappa, keep, range(owned, owned + NVAR), rows)
    for j in range(lane_tiles):
        for v in range(NVAR):
            out_static[v, :, columns[j]] = static[v, :, columns[j]] + adj4[owned + v, j, own, :] * inverse[j]
    wait(adj_pair)
    for j in range(lane_tiles):
        for f in range(owned):
            unpack(adj_recv, f * lane_tiles + j, adj0, (f, j))
    border_rows(adj, kappa, keep, range(owned), rows)
    for j in range(lane_tiles):
        for f in range(owned):
            out_alpha[f, :, columns[j]] = alpha[f, :, columns[j]] + adj4[f, j, own, :] * inverse[j]


def write_out(alpha, static, out_alpha, out_static, sems):
    owned = alpha.shape[0]
    copies = [pltpu.make_async_copy(static.at[v], out_static.at[v], sems.at[owned + v]) for v in range(NVAR)]
    copies += [pltpu.make_async_copy(alpha.at[f], out_alpha.at[f], sems.at[f]) for f in range(owned)]
    for copy in copies:
        copy.start()
    for copy in copies:
        copy.wait()


def body(tiles, members, alpha_fields, static_control, perturbations, coef_table, coef_class, obs_cells, obs_counts, innovations, obs_weights):
    owned, rows, cols = alpha_fields.shape
    slots = obs_cells.shape[1] // LANES
    folded = (slots, LANES)
    half = slots // 2
    depth = members // 4
    fields = owned + NVAR
    lane_tiles = cols // LANES
    deep = rows + 2 * PAD
    field_rows = cols // WIDE * NVAR * rows
    f32, bf16, i32 = jnp.float32, jnp.bfloat16, jnp.int32
    anywhere = pl.BlockSpec(memory_space=pl.ANY)
    in_hbm = functools.partial(pltpu.with_memory_space_constraint, memory_space=pltpu.HBM)
    in_vmem = pl.BlockSpec(memory_space=pltpu.VMEM)
    dma = pltpu.SemaphoreType.DMA

    def message(count):
        return [pltpu.VMEM((2, count * lane_tiles // 2, 8, LANES), f32)] * 2

    shapes = (jax.ShapeDtypeStruct((owned, rows, cols), f32), jax.ShapeDtypeStruct((NVAR, rows, cols), f32))
    grads = pl.pallas_call(
        functools.partial(kernel, tiles, members),
        out_shape=shapes,
        in_specs=[anywhere] * 9,
        out_specs=(in_vmem, in_vmem),
        scratch_shapes=[
            pltpu.VMEM((owned, rows, cols), f32),
            pltpu.VMEM((NVAR, rows, cols), f32),
            pltpu.VMEM((owned, NVAR, rows, cols), bf16),
            pltpu.VMEM((rows, cols), i32),
            pltpu.VMEM(folded, i32),
            pltpu.VMEM(folded, f32),
            pltpu.VMEM(folded, f32),
            pltpu.SMEM(coef_table.shape, f32),
            pltpu.SMEM(obs_counts.shape, i32),
            pltpu.VMEM((lane_tiles, deep, LANES), f32),
            pltpu.VMEM((lane_tiles, deep, LANES), f32),
            pltpu.VMEM((lane_tiles, rows, LANES), f32),
            *[pltpu.VMEM((owned + 1, lane_tiles, deep, LANES), f32)] * (STEPS + 1),
            *[pltpu.VMEM((fields, lane_tiles, deep, LANES), f32)] * (STEPS + 1),
            *message(owned + 1),
            *message(1),
            *message(NVAR),
            *message(owned),
            pltpu.VMEM((field_rows, WIDE), f32),
            pltpu.VMEM((2, field_rows, WIDE), bf16),
            pltpu.VMEM((WIDE, slots * LANES), bf16),
            pltpu.VMEM((field_rows, slots * LANES), bf16),
            pltpu.VMEM(folded, f32),
            pltpu.VMEM((4, half, LANES), f32),
            pltpu.VMEM((depth, half, LANES), f32),
            pltpu.VMEM(folded, f32),
            dma((9,)),
            dma((2, 2)),
            dma((2, 2)),
            dma((2, 2)),
            dma((2, 2)),
            dma((2, 4)),
            dma((2, depth)),
            dma((2,)),
        ],
        compiler_params=pltpu.CompilerParams(collective_id=0, has_side_effects=True, vmem_limit_bytes=48 * 2**20),
    )(
        in_hbm(alpha_fields),
        in_hbm(static_control),
        in_hbm(perturbations),
        in_hbm(coef_table),
        in_hbm(coef_class),
        in_hbm(obs_cells.reshape(folded)),
        obs_counts,
        in_hbm(innovations.reshape(folded)),
        in_hbm(obs_weights.reshape(folded)),
    )
    return pl.pallas_call(
        write_out,
        out_shape=shapes,
        in_specs=[anywhere, anywhere],
        out_specs=(anywhere, anywhere),
        scratch_shapes=[dma((fields,))],
        compiler_params=pltpu.CompilerParams(vmem_limit_bytes=2**20),
    )(*grads)


def solution(mesh):
    in_specs = (
        P("mem", "tile", None),
        P(None, "tile", None),
        P("mem", None, "tile", None),
        P(),
        P("tile", None),
        P("tile", None),
        P("tile"),
        P("tile", None),
        P("tile", None),
    )
    out_specs = (P("mem", "tile", None), P(None, "tile", None))
    run = functools.partial(body, mesh.shape["tile"], mesh.shape["mem"])
    return jax.shard_map(run, mesh=mesh, in_specs=in_specs, out_specs=out_specs, check_vma=False)
```
